512 devices in a mesh: band: 64 (over z, y), mp: 8 (over x, core).
Axes of the slice: x: 4, y: 8, z: 8, core: 2. Of those that a mesh axis runs over, the one named last changes fastest.
Arguments:
- grid_latent: bfloat16 [262144, 1024], P(('band', 'mp')), may hold values from -6 to 6
- grid_gain: float32 [1024], replicated, may hold values from 0.1 to 1.9
- hidden_in: bfloat16 [16384, 1024], P('band'), may hold values from -6 to 6
- hid_gain: float32 [1024], replicated, may hold values from 0.1 to 1.9
- enc_wq: bfloat16 [1024, 1024], P(None, 'mp'), may hold values from -8 to 8
- enc_wk: bfloat16 [1024, 1024], P(None, 'mp'), may hold values from -0.1875 to 0.1875
- enc_wv: bfloat16 [1024, 1024], P(None, 'mp'), may hold values from -0.1875 to 0.1875
- enc_wo: bfloat16 [1024, 1024], P('mp'), may hold values from -0.1875 to 0.1875
- enc_edges: int32 [16384, 32], P('band'), may hold values from 0 to 262143, as said below
- enc_counts: int32 [16384], P('band'), may hold values from 1 to 32
- proc_gain: float32 [1024], replicated, may hold values from 0.1 to 1.9
- proc_wq: bfloat16 [1024, 1024], P(None, 'mp'), may hold values from -8 to 8
- proc_wk: bfloat16 [1024, 1024], P(None, 'mp'), may hold values from -0.25 to 0.25
- proc_wv: bfloat16 [1024, 1024], P(None, 'mp'), may hold values from -0.1875 to 0.1875
- proc_wo: bfloat16 [1024, 1024], P('mp'), may hold values from -0.1875 to 0.1875
Outputs:
- mixed: bfloat16 [16384, 1024], P('band')
The draws below stay inside these ranges and needn't reach their ends.
Inputs may be any that keep to these rules, and one draw needn't show every extreme that they name: `enc_edges`: node n lies in band b = n // 256; each of its edges references a grid point from b * 4096 - 512 to (b + 1) * 4096 + 511. Slots at or beyond the node's count hold valid grid points as well.
All inputs are finite; a program needn't handle non-finite values.
Results may differ from the reference program's by a relative error of at most 0.02.
Values may be sent and summed in bfloat16 or wider, within the bound.
A program may use at most 64 MiB of HBM per device.

```python
import jax
import jax.numpy as jnp
from jax import lax

D = 1024
HEADS = 16
K_SLOTS = 32
WIN = 128
NODE_BAND = 256
GRID_BAND = 4096
GRID = 262144
RIM = 512
NODES = 16384
N_BAND = 64
N_MP = 8


def draw_enc_edges(key, part):
    nodes = jnp.arange(NODES, dtype=jnp.int32)
    band = nodes // NODE_BAND
    slot = jnp.arange(K_SLOTS, dtype=jnp.int32)
    rim_offset = jax.random.randint(jax.random.fold_in(key, 3), (NODES, K_SLOTS), 0, RIM, dtype=jnp.int32)
    band_offset = jax.random.randint(jax.random.fold_in(key, 4), (NODES, K_SLOTS), 0, GRID_BAND, dtype=jnp.int32)
    lower = band[:, None] * GRID_BAND - RIM + rim_offset
    upper = (band[:, None] + 1) * GRID_BAND + rim_offset
    inside = band[:, None] * GRID_BAND + band_offset
    kind = (slot % 4)[None, :]
    chosen = jnp.where(kind == 0, lower, jnp.where(kind == 2, upper, inside))
    return jnp.clip(chosen, 0, GRID - 1).astype(jnp.int32)


def draw_enc_counts(key, part):
    counts = jax.random.randint(jax.random.fold_in(key, 5), (NODES,), 1, K_SLOTS + 1, dtype=jnp.int32)
    spot = jax.random.randint(jax.random.fold_in(key, 6), (), 0, NODES, dtype=jnp.int32)
    return jnp.where(jnp.arange(NODES, dtype=jnp.int32) == spot, K_SLOTS, counts).astype(jnp.int32)


def draw_enc_wq(key, part):
    drawn = jax.random.normal(jax.random.fold_in(key, 29), (D, D), jnp.float32) * D ** (-0.5)
    return jnp.clip(drawn, -8.0, 8.0).astype(jnp.bfloat16)


def shared_keys(key):
    return jax.random.normal(jax.random.fold_in(key, 17), (D, D), jnp.float32) * D ** (-0.5)


def draw_proc_wk(key, part):
    return jnp.clip(shared_keys(key), -0.25, 0.25).astype(jnp.bfloat16)


def draw_proc_wq(key, part):
    drawn = jax.random.normal(jax.random.fold_in(key, 23), (D, D), jnp.float32) * D ** (-0.5)
    return jnp.clip(drawn, -8.0, 8.0).astype(jnp.bfloat16)


def level_of(key, shape, cuts, low, high):
    def one(position, parts):
        steps = jax.random.uniform(jax.random.fold_in(jax.random.fold_in(key, 6), position), (parts,), jnp.float32, low / len(cuts), high / len(cuts))
        return jnp.repeat(jnp.exp(steps), shape[position] // parts).reshape((-1,) + (1,) * (len(shape) - position - 1))

    level = one(*cuts[0])
    for cut in cuts[1:]:
        level = level * one(*cut)
    return level


def noise(key, extent, scale, reach, cuts=(), kind=jnp.bfloat16):
    values = jax.random.normal(key, extent, jnp.float32) * scale
    if len(cuts) > 0:
        values = level_of(key, extent, cuts, -0.22, 0.18) * values
    return jnp.clip(values, min=-reach, max=reach).astype(kind)


def setup_inputs(seed: int = 0) -> dict:
    key_of = jax.random.split(jax.random.key(seed), 16)
    grid_latent = noise(key_of[0], (GRID, D), 1.0, 6.0, ((0, 512),))
    grid_gain = jnp.clip(1.0 + 0.18 * jax.random.normal(key_of[1], (D,), jnp.float32), 0.1, 1.9)
    hidden_in = noise(key_of[2], (NODES, D), 1.0, 6.0, ((0, 64),))
    hid_gain = jnp.clip(1.0 + 0.18 * jax.random.normal(key_of[3], (D,), jnp.float32), 0.1, 1.9)
    enc_wq = draw_enc_wq(jax.random.fold_in(key_of[15], 71), 0)
    enc_wk = noise(key_of[5], (D, D), D ** -0.5, 0.1875, ((1, 8),))
    enc_wv = noise(key_of[6], (D, D), D ** -0.5, 0.1875, ((1, 8),))
    enc_wo = noise(key_of[7], (D, D), D ** -0.5, 0.1875, ((0, 8),))
    enc_edges = draw_enc_edges(jax.random.fold_in(key_of[15], 71), 0)
    enc_counts = draw_enc_counts(jax.random.fold_in(key_of[15], 71), 0)
    proc_gain = jnp.clip(1.0 + 0.18 * jax.random.normal(key_of[10], (D,), jnp.float32), 0.1, 1.9)
    proc_wq = draw_proc_wq(jax.random.fold_in(key_of[15], 71), 0)
    proc_wk = draw_proc_wk(jax.random.fold_in(key_of[15], 71), 0)
    proc_wv = noise(key_of[13], (D, D), D ** -0.5, 0.1875, ((1, 8),))
    proc_wo = noise(key_of[14], (D, D), D ** -0.5, 0.1875, ((0, 8),))
    return {"grid_latent": grid_latent, "grid_gain": grid_gain, "hidden_in": hidden_in, "hid_gain": hid_gain, "enc_wq": enc_wq, "enc_wk": enc_wk, "enc_wv": enc_wv, "enc_wo": enc_wo, "enc_edges": enc_edges, "enc_counts": enc_counts, "proc_gain": proc_gain, "proc_wq": proc_wq, "proc_wk": proc_wk, "proc_wv": proc_wv, "proc_wo": proc_wo}


EPSILON = 1e-05

def layer_norm(values, gain):
    values = values.astype(jnp.float32)
    center = values - lax.optimization_barrier(jnp.mean(values, axis=-1, keepdims=True))
    spread = lax.optimization_barrier(jnp.mean(center * center, axis=-1, keepdims=True))
    return center * lax.rsqrt(spread + EPSILON) * gain

def softmax_rows(scores):
    top = lax.optimization_barrier(jnp.max(scores, axis=-1, keepdims=True))
    expd = jnp.exp(scores - top)
    return (expd / lax.optimization_barrier(jnp.sum(expd, axis=-1, keepdims=True))).astype(jnp.bfloat16)

def edge_attention(query, keys, values, valid):
    scale = query.shape[-1] ** (-0.5)
    scores = jnp.einsum('nhe,nshe->nhs', query.astype(jnp.float32), keys.astype(jnp.float32)) * scale
    scores = jnp.where(valid[:, None, :], scores, -jnp.inf)
    weights = softmax_rows(scores)
    out = jnp.einsum('nhs,nshe->nhe', weights.astype(jnp.float32), values.astype(jnp.float32))
    return out.astype(jnp.bfloat16)

def window_attention(query, keys, values, valid):
    scale = query.shape[-1] ** (-0.5)
    scores = jnp.einsum('nhe,mhe->nhm', query.astype(jnp.float32), keys.astype(jnp.float32)) * scale
    scores = jnp.where(valid[:, None, :], scores, -jnp.inf)
    weights = softmax_rows(scores)
    out = jnp.einsum('nhm,mhe->nhe', weights.astype(jnp.float32), values.astype(jnp.float32))
    return out.astype(jnp.bfloat16)

def head_sum(heads, w_out, groups):
    count = heads.shape[0]
    width = heads.shape[1] // groups
    pieces = heads.reshape(count, groups, width).astype(jnp.float32)
    blocks = w_out.reshape(groups, width, -1).astype(jnp.float32)
    partial_value = jnp.einsum('npc,pcd->npd', pieces, blocks).astype(jnp.bfloat16)
    return lax.optimization_barrier(jnp.sum(partial_value.astype(jnp.float32), axis=1))

def project(rows, weight):
    return jnp.dot(rows, weight, preferred_element_type=jnp.float32).astype(jnp.bfloat16)

def reference(grid_latent, grid_gain, hidden_in, hid_gain, enc_wq, enc_wk, enc_wv, enc_wo, enc_edges, enc_counts, proc_gain, proc_wq, proc_wk, proc_wv, proc_wo):
    head_dim = D // HEADS
    grid_norm = layer_norm(grid_latent, grid_gain).astype(jnp.bfloat16)
    enc_keys = project(grid_norm, enc_wk)
    enc_values = project(grid_norm, enc_wv)
    node_norm = layer_norm(hidden_in, hid_gain).astype(jnp.bfloat16)
    enc_query = project(node_norm, enc_wq)

    def encode_band(band):
        start = (band * NODE_BAND).astype(jnp.int32)
        rows = lax.dynamic_slice_in_dim(enc_query, start, NODE_BAND, 0).reshape(NODE_BAND, HEADS, head_dim)
        edges = lax.dynamic_slice_in_dim(enc_edges, start, NODE_BAND, 0).reshape(-1)
        counts = lax.dynamic_slice_in_dim(enc_counts, start, NODE_BAND, 0)
        near_keys = jnp.take(enc_keys, edges, axis=0).reshape(NODE_BAND, K_SLOTS, HEADS, head_dim)
        near_values = jnp.take(enc_values, edges, axis=0).reshape(NODE_BAND, K_SLOTS, HEADS, head_dim)
        valid = jnp.arange(K_SLOTS, dtype=jnp.int32)[None, :] < counts[:, None]
        heads = edge_attention(rows, near_keys, near_values, valid).reshape(NODE_BAND, D)
        base = lax.dynamic_slice_in_dim(hidden_in, start, NODE_BAND, 0).astype(jnp.float32)
        return base + head_sum(heads, enc_wo, N_MP)
    latent = lax.map(encode_band, jnp.arange(N_BAND, dtype=jnp.int32)).reshape(NODES, D)
    proc_norm = layer_norm(latent, proc_gain).astype(jnp.bfloat16)
    proc_query = project(proc_norm, proc_wq)
    proc_keys = project(proc_norm, proc_wk)
    proc_values = project(proc_norm, proc_wv)
    margin = jnp.zeros((WIN, D), jnp.bfloat16)
    keys_wide = jnp.concatenate([margin, proc_keys, margin], axis=0)
    values_wide = jnp.concatenate([margin, proc_values, margin], axis=0)
    span = NODE_BAND + 2 * WIN

    def window_band(band):
        start = (band * NODE_BAND).astype(jnp.int32)
        rows = lax.dynamic_slice_in_dim(proc_query, start, NODE_BAND, 0).reshape(NODE_BAND, HEADS, head_dim)
        keys = lax.dynamic_slice_in_dim(keys_wide, start, span, 0).reshape(span, HEADS, head_dim)
        values = lax.dynamic_slice_in_dim(values_wide, start, span, 0).reshape(span, HEADS, head_dim)
        own = start + jnp.arange(NODE_BAND, dtype=jnp.int32)
        other = start - WIN + jnp.arange(span, dtype=jnp.int32)
        valid = (jnp.abs(own[:, None] - other[None, :]) <= WIN) & (other >= 0)[None, :] & (other < NODES)[None, :]
        heads = window_attention(rows, keys, values, valid).reshape(NODE_BAND, D)
        base = lax.dynamic_slice_in_dim(latent, start, NODE_BAND, 0)
        return (base + head_sum(heads, proc_wo, N_MP)).astype(jnp.bfloat16)
    return lax.map(window_band, jnp.arange(N_BAND, dtype=jnp.int32)).reshape(NODES, D)
```

```python
import functools

import jax
import jax.numpy as jnp
from jax import lax
from jax.experimental import pallas as pl
from jax.experimental.pallas import tpu as pltpu
from jax.sharding import PartitionSpec as P

MESH = pl.DeviceIdType.MESH
EPSILON = 1e-05
NEG = -1e30
F32 = jnp.float32
BF16 = jnp.bfloat16

D = 1024
CHIPS = 4
ROWS = 512
NODES = 256
SLOTS = 32
WIN = 128
COLS = 128
HALF = 64
OWN = NODES // CHIPS


def norm_rows(values, gain):
    values = values.astype(F32)
    center = values - jnp.mean(values, axis=-1, keepdims=True)
    spread = jnp.mean(center * center, axis=-1, keepdims=True)
    return center * lax.rsqrt(spread + EPSILON) * gain


def at_cols(start):
    return pl.ds(pl.multiple_of(start, COLS), COLS)


class Ring:
    def __init__(self, place, own, send, recv):
        self.place, self.own, self.send, self.recv = place, own, send, recv

    def bind(self, x, c):
        self.x, self.c = x, c
        self.left, self.right = lax.rem(x + 3, 4), lax.rem(x + 1, 4)
        self.far = lax.rem(x + 2, 4)
        return self

    def copy(self, source, c, x, half, kind):
        target = (2 * self.right + self.c, 2 * self.left + self.c, 2 * self.x + 1 - self.c)[kind]
        return pltpu.make_async_remote_copy(
            src_ref=source,
            dst_ref=self.place(c, x, half),
            send_sem=self.send.at[kind, x, half],
            recv_sem=self.recv.at[c, x, half],
            device_id={"mp": target},
            device_id_type=MESH,
        )

    def held(self, c, x, half, kind):
        return self.copy(self.place(c, x, half), c, x, half, kind)

    def start(self):
        for half in range(2):
            for kind in range(2):
                self.copy(self.own(half), self.c, self.x, half, kind).start()

    def start_partner(self):
        for half in range(2):
            self.copy(self.own(half), self.c, self.x, half, 2).start()

    def arrived(self, x):
        for half in range(2):
            self.held(self.c, x, half, 2).wait_recv()

    def pass_on(self, x):
        for half in range(2):
            self.held(self.c, x, half, 2).start()

    def relay_left(self, partner):
        self.arrived(self.left)
        self.held(self.c, self.left, 0, 0).start()
        if partner:
            self.pass_on(self.left)

    def relay_right(self, partner):
        self.arrived(self.right)
        self.held(self.c, self.right, 1, 1).start()
        if partner:
            self.pass_on(self.right)

    def relay_far(self, partner):
        self.arrived(self.far)
        if partner:
            self.pass_on(self.far)

    def from_partner(self):
        for x in range(4):
            for half in range(2):
                self.held(1 - self.c, x, half, 2).wait_recv()

    def drain(self, partner):
        for half in range(2):
            for kind in range(2):
                self.copy(self.own(half), self.c, self.x, half, kind).wait_send()
        self.held(self.c, self.left, 0, 0).wait_send()
        self.held(self.c, self.right, 1, 1).wait_send()
        if partner:
            for half in range(2):
                self.copy(self.own(half), self.c, self.x, half, 2).wait_send()
                for x in (self.left, self.right, self.far):
                    self.held(self.c, x, half, 2).wait_send()


def fill_bias(edges_ref, counts_ref, bias_ref, base, width):
    step = 16
    slot = lax.broadcasted_iota(jnp.int32, (step, SLOTS), 1)
    column = lax.broadcasted_iota(jnp.int32, (step, width), 1)
    lane = lax.broadcasted_iota(jnp.int32, (step, NODES), 1)
    row = lax.broadcasted_iota(jnp.int32, (step, NODES), 0)

    def block(i, carry):
        at = pl.multiple_of(i * step, step)
        picked = jnp.where(lane == row + at, counts_ref[...], 0)
        count = jnp.sum(picked, axis=1, keepdims=True)
        edges = jnp.where(slot < count, edges_ref[pl.ds(at, step), :] - base, -1)
        total = jnp.zeros((step, width), F32)
        for s in range(SLOTS):
            total = total + jnp.where(edges[:, s : s + 1] == column, 1.0, 0.0)
        bias_ref[pl.ds(at, step), :] = jnp.where(
            total > 0.0, jnp.log(jnp.maximum(total, 1.0)), NEG
        )
        return carry

    lax.fori_loop(0, NODES // step, block, 0)


def two_heads(query, keys, values, bias):
    first = lax.broadcasted_iota(jnp.int32, query.shape, 1) < HALF
    outs, sums = [], []
    for h in range(2):
        q = jnp.where(first if h == 0 else jnp.logical_not(first), query, jnp.zeros_like(query))
        scores = lax.dot_general(q, keys, (((1,), (1,)), ((), ())), preferred_element_type=F32) + bias
        top = jnp.max(scores, axis=1, keepdims=True)
        weights = jnp.exp(scores - top).astype(BF16)
        both = jnp.dot(weights, values, preferred_element_type=F32)
        total = both[:, COLS:]
        outs.append(both[:, :COLS] / total)
        sums.append(top + jnp.log(total))
    return jnp.where(first, outs[0], outs[1]).astype(BF16), sums


def kernel(
    bands,
    grid, wk, wv, wo, pwk, pwv, pwq, pwo, edges_hbm, counts_hbm,
    grid_gain, hidden, hid_gain, wq, edges, counts, proc_gain,
    out,
    raw, normed, node, w, q, qr, keys, vals, bias, bias_r, edges_r, counts_r,
    part, stat, part_r, stat_r, po, st, heads, wo_all, pwo_all, latent, pw, pq, kvp, heads2,
    ks, kr, vs, vr, os, orr, ps, pr, hs, hr, gs, gr,
    loc, grid_sem, edge_sem, q_send, q_recv, qr_send, qr_recv,
    po_send, po_recv, st_send, st_recv, ro_send, rs_send, kv_send, kv_recv,
):
    b, m = lax.axis_index("band"), lax.axis_index("mp")
    x, c = lax.div(m, 2), lax.rem(m, 2)
    up, down = lax.rem(b + 1, bands), lax.rem(b + bands - 1, bands)
    is_top, is_low = x == 3, x == 0
    is_rim = jnp.logical_or(is_top, is_low)

    barrier = pltpu.get_barrier_semaphore()
    for d in range(1, 8):
        pl.semaphore_signal(barrier, inc=1, device_id={"mp": lax.rem(m + d, 8)}, device_id_type=MESH)
    for band in (up, down):
        for d in range(4):
            pl.semaphore_signal(
                barrier, inc=1, device_id={"band": band, "mp": 2 * d + c}, device_id_type=MESH
            )

    slot = c * 4 + x
    local = [
        pltpu.make_async_copy(wk, w.at[x, :, 0:COLS], loc.at[0]),
        pltpu.make_async_copy(wv, w.at[x, :, COLS:], loc.at[1]),
        pltpu.make_async_copy(grid, raw.at[pl.ds(pl.multiple_of(c * ROWS, ROWS), ROWS), :], loc.at[2]),
        pltpu.make_async_copy(wo, wo_all.at[pl.ds(pl.multiple_of(slot * COLS, COLS), COLS), :], loc.at[3]),
        pltpu.make_async_copy(pwo, pwo_all.at[pl.ds(pl.multiple_of(slot * COLS, COLS), COLS), :], loc.at[4]),
        pltpu.make_async_copy(pwk, pw.at[:, 0:COLS], loc.at[5]),
        pltpu.make_async_copy(pwv, pw.at[:, COLS:], loc.at[6]),
        pltpu.make_async_copy(pwq, pq, loc.at[7]),
    ]
    for one in local:
        one.start()
    pl.semaphore_wait(barrier, 15)

    def rows_of(ref, half):
        return ref.at[pl.ds(half * (D // 2), D // 2), :]

    ring_k = Ring(
        lambda cc, xx, half: w.at[xx, pl.ds(half * (D // 2), D // 2), pl.ds(0, COLS)],
        lambda half: rows_of(wk, half), ks, kr,
    ).bind(x, c)
    ring_v = Ring(
        lambda cc, xx, half: w.at[xx, pl.ds(half * (D // 2), D // 2), pl.ds(COLS, COLS)],
        lambda half: rows_of(wv, half), vs, vr,
    ).bind(x, c)

    def eighth(ref):
        return lambda cc, xx, half: ref.at[
            pl.ds(pl.multiple_of((cc * 4 + xx) * COLS + half * HALF, HALF), HALF), :
        ]

    ring_o = Ring(eighth(wo_all), lambda half: wo.at[pl.ds(half * HALF, HALF), :], os, orr).bind(x, c)
    ring_p = Ring(eighth(pwo_all), lambda half: pwo.at[pl.ds(half * HALF, HALF), :], ps, pr).bind(x, c)

    def head_piece(cc, xx, half):
        return heads.at[
            pl.ds(pl.multiple_of(xx * OWN + half * (OWN // 2), OWN // 2), OWN // 2),
            pl.ds(pl.multiple_of(cc * 512, 512), 512),
        ]

    ring_h = Ring(head_piece, lambda half: head_piece(c, x, half), hs, hr).bind(x, c)

    def out_piece(cc, xx, half):
        return heads2.at[pl.ds(half * 128, 128), at_cols((cc * 4 + xx) * COLS)]

    ring_g = Ring(out_piece, lambda half: out_piece(c, x, half), gs, gr).bind(x, c)

    ring_k.start()
    ring_v.start()
    grid_own = pl.ds(pl.multiple_of(c * ROWS, ROWS), ROWS)
    grid_other = pl.ds(pl.multiple_of((1 - c) * ROWS, ROWS), ROWS)
    to_partner = pltpu.make_async_remote_copy(
        src_ref=grid, dst_ref=raw.at[grid_own, :], send_sem=grid_sem.at[0], recv_sem=grid_sem.at[1],
        device_id={"mp": 2 * x + 1 - c}, device_id_type=MESH,
    )
    to_partner.start()

    def rim_input(source, target, k, band):
        return pltpu.make_async_remote_copy(
            src_ref=source, dst_ref=target, send_sem=edge_sem.at[0, k], recv_sem=edge_sem.at[1, k],
            device_id={"band": band, "mp": m}, device_id_type=MESH,
        )

    rim_from = jnp.where(is_top, down, up)
    rim_to = jnp.where(is_top, up, down)
    edge_copies = [
        rim_input(edges_hbm, edges_r, 0, rim_from),
        rim_input(counts_hbm, counts_r, 1, rim_from),
    ]

    @pl.when(is_rim)
    def _():
        for one in edge_copies:
            one.start()

    def node_block(i, carry):
        at = pl.ds(pl.multiple_of(i * 64, 64), 64)
        node[at, :] = norm_rows(hidden[at, :], hid_gain[...]).astype(BF16)
        return carry

    lax.fori_loop(0, NODES // 64, node_block, 0)
    q[x] = jnp.dot(node[...], wq[...], preferred_element_type=F32).astype(BF16) * BF16(0.125)

    def q_copy(d):
        return pltpu.make_async_remote_copy(
            src_ref=q.at[x], dst_ref=q.at[x], send_sem=q_send.at[d], recv_sem=q_recv.at[x],
            device_id={"mp": 2 * lax.rem(x + d + 1, 4) + c}, device_id_type=MESH,
        )

    def qr_copy(k):
        return pltpu.make_async_remote_copy(
            src_ref=q.at[x], dst_ref=qr.at[x], send_sem=qr_send.at[k], recv_sem=qr_recv.at[x],
            device_id={"band": (down, up)[k], "mp": (6, 0)[k] + c}, device_id_type=MESH,
        )

    def q_arrival(ref, sems, xx):
        return pltpu.make_async_remote_copy(
            src_ref=ref.at[xx], dst_ref=ref.at[xx], send_sem=q_send.at[0], recv_sem=sems.at[xx],
            device_id={"mp": 2 * xx + c}, device_id_type=MESH,
        )

    for d in range(3):
        q_copy(d).start()
    for k in range(2):
        qr_copy(k).start()

    def grid_block(i, carry):
        at = pl.ds(pl.multiple_of(i * 64, 64), 64)
        normed[at, :] = norm_rows(raw[at, :], grid_gain[...]).astype(BF16)
        return carry

    local[2].wait()
    lax.fori_loop(c * 8, c * 8 + 8, grid_block, 0)

    base = b * (8 * ROWS) + x * (2 * ROWS)
    rim_row = jnp.where(is_top, ROWS, 0)
    fill_bias(edges, counts, bias, base, 2 * ROWS)
    vals[:, COLS:] = jnp.ones((2 * ROWS, COLS), BF16)
    stat[...] = jnp.zeros_like(stat)
    stat_r[...] = jnp.zeros_like(stat_r)

    pltpu.make_async_remote_copy(
        src_ref=grid, dst_ref=raw.at[grid_other, :], send_sem=grid_sem.at[0], recv_sem=grid_sem.at[1],
        device_id={"mp": 2 * x + 1 - c}, device_id_type=MESH,
    ).wait_recv()
    lax.fori_loop((1 - c) * 8, (1 - c) * 8 + 8, grid_block, 0)

    @pl.when(is_rim)
    def _():
        for one in edge_copies:
            one.wait_recv()
        fill_bias(edges_r, counts_r, bias_r, base + rim_row, ROWS)

    def part_copy(xs, d):
        xx = lax.rem(x + d + 1, 4)
        return pltpu.make_async_remote_copy(
            src_ref=part.at[xs, pl.ds(pl.multiple_of(xx * OWN, OWN), OWN), :],
            dst_ref=po.at[x, xs],
            send_sem=po_send.at[d, xs], recv_sem=po_recv.at[x, xs],
            device_id={"mp": 2 * xx + c}, device_id_type=MESH,
        )

    rim_slot = jnp.where(is_top, 4, 5)

    def rim_copy(xs, xx):
        return pltpu.make_async_remote_copy(
            src_ref=part_r.at[xs, pl.ds(xx * OWN, OWN), :],
            dst_ref=po.at[rim_slot, xs],
            send_sem=ro_send.at[xx, xs], recv_sem=po_recv.at[rim_slot, xs],
            device_id={"band": rim_to, "mp": 2 * xx + c}, device_id_type=MESH,
        )

    def stat_copy(d):
        xx = lax.rem(x + d + 1, 4)
        return pltpu.make_async_remote_copy(
            src_ref=stat.at[pl.ds(pl.multiple_of(xx * OWN, OWN), OWN), :],
            dst_ref=st.at[x],
            send_sem=st_send.at[d], recv_sem=st_recv.at[x],
            device_id={"mp": 2 * xx + c}, device_id_type=MESH,
        )

    def rim_stat_copy(xx):
        return pltpu.make_async_remote_copy(
            src_ref=stat_r.at[pl.ds(xx * OWN, OWN), :],
            dst_ref=st.at[rim_slot],
            send_sem=rs_send.at[xx], recv_sem=st_recv.at[rim_slot],
            device_id={"band": rim_to, "mp": 2 * xx + c}, device_id_type=MESH,
        )

    chunk = 128

    def attend(xs, q_ref, bias_ref, part_ref, stat_ref, first_row, width):
        def block(i, carry):
            at = pl.ds(pl.multiple_of(i * chunk, chunk), chunk)
            span = pl.ds(pl.multiple_of(first_row, ROWS), width)
            result, sums = two_heads(q_ref[xs, at, :], keys[span, :], vals[span, :], bias_ref[at, :])
            part_ref[xs, at, :] = result
            lane = lax.broadcasted_iota(jnp.int32, (chunk, 128), 1)
            old = stat_ref[at, :]
            old = jnp.where(lane == 2 * xs, sums[0], old)
            stat_ref[at, :] = jnp.where(lane == 2 * xs + 1, sums[1], old)
            return carry

        lax.fori_loop(0, NODES // chunk, block, 0)

    def head_step(j, carry):
        xs = lax.rem(x + jnp.where(j == 0, 0, jnp.where(j == 1, 3, jnp.where(j == 2, 1, 2))), 4)

        @pl.when(j == 0)
        def _():
            local[0].wait()
            local[1].wait()

        @pl.when(j == 1)
        def _():
            for ring in (ring_k, ring_v):
                ring.relay_left(False)
            for ring in (ring_k, ring_v):
                ring.relay_right(False)
            ring_o.start()
            ring_o.start_partner()

        @pl.when(j == 3)
        def _():
            for ring in (ring_k, ring_v):
                ring.relay_far(False)

        @pl.when(j > 0)
        def _():
            q_arrival(q, q_recv, xs).wait_recv()

        def project(i, inner):
            at = pl.ds(pl.multiple_of(i * ROWS, ROWS), ROWS)
            both = jnp.dot(normed[at, :], w[xs], preferred_element_type=F32).astype(BF16)
            keys[at, :] = both[:, :COLS]
            vals[at, 0:COLS] = both[:, COLS:]
            return inner

        lax.fori_loop(0, 2, project, 0)

        @pl.when(is_rim)
        def _():
            q_arrival(qr, qr_recv, xs).wait_recv()
            attend(xs, qr, bias_r, part_r, stat_r, rim_row, ROWS)
            for xx in range(4):
                rim_copy(xs, xx).start()

        attend(xs, q, bias, part, stat, 0, 2 * ROWS)
        for d in range(3):
            part_copy(xs, d).start()
        return carry

    lax.fori_loop(0, 4, head_step, 0)

    for d in range(3):
        stat_copy(d).start()

    @pl.when(is_rim)
    def _():
        for xx in range(4):
            rim_stat_copy(xx).start()

    mine = pl.ds(pl.multiple_of(x * OWN, OWN), OWN)
    st[x] = stat[mine, :]
    for xs in range(4):
        po[x, xs] = part[xs, mine, :]
    ring_o.relay_left(True)
    ring_o.relay_right(True)

    def arrivals(i):
        for xs in range(4):
            pltpu.make_async_remote_copy(
                src_ref=po.at[i, xs], dst_ref=po.at[i, xs],
                send_sem=po_send.at[0, xs], recv_sem=po_recv.at[i, xs],
                device_id={"mp": m}, device_id_type=MESH,
            ).wait_recv()
        pltpu.make_async_remote_copy(
            src_ref=st.at[i], dst_ref=st.at[i], send_sem=st_send.at[0], recv_sem=st_recv.at[i],
            device_id={"mp": m}, device_id_type=MESH,
        ).wait_recv()

    for d in range(3):
        arrivals(lax.rem(x + d + 1, 4))
    arrivals(4)
    arrivals(5)

    top = st[0]
    for i in range(1, 6):
        top = jnp.maximum(top, st[i])
    shares = [jnp.exp(st[i] - top) for i in range(6)]
    whole = shares[0]
    for i in range(1, 6):
        whole = whole + shares[i]
    shares = [one / whole for one in shares]
    first = lax.broadcasted_iota(jnp.int32, (OWN, COLS), 1) < HALF
    for xs in range(4):
        total = jnp.zeros((OWN, COLS), F32)
        for i in range(6):
            left = jnp.broadcast_to(shares[i][:, 2 * xs : 2 * xs + 1], (OWN, COLS))
            right = jnp.broadcast_to(shares[i][:, 2 * xs + 1 : 2 * xs + 2], (OWN, COLS))
            total = total + jnp.where(first, left, right) * po[i, xs].astype(F32)
        heads[mine, at_cols(c * 512 + xs * COLS)] = total.astype(BF16)

    ring_h.start()
    ring_h.start_partner()
    ring_h.relay_left(True)
    ring_h.relay_right(True)
    ring_h.relay_far(True)
    ring_p.start()
    ring_p.start_partner()
    ring_o.relay_far(True)
    local[3].wait()
    ring_o.from_partner()
    ring_h.from_partner()

    def latent_block(n, carry):
        at = pl.ds(pl.multiple_of(n * 256, 256), 256)
        latent[:, at] = hidden[:, at].astype(F32) + jnp.dot(
            heads[...], wo_all[:, at], preferred_element_type=F32
        )
        return carry

    lax.fori_loop(0, 4, latent_block, 0)

    def latent_norm(i, carry):
        at = pl.ds(pl.multiple_of(i * 64, 64), 64)
        node[at, :] = norm_rows(latent[at, :], proc_gain[...]).astype(BF16)
        return carry

    lax.fori_loop(0, NODES // 64, latent_norm, 0)

    local[5].wait()
    local[6].wait()
    kvp[WIN : WIN + NODES, :] = jnp.dot(
        node[...], pw[...], preferred_element_type=F32
    ).astype(BF16)

    def kv_copy(k):
        source, target = ((NODES, 0), (WIN, WIN + NODES))[k]
        return pltpu.make_async_remote_copy(
            src_ref=kvp.at[pl.ds(source, WIN), :], dst_ref=kvp.at[pl.ds(target, WIN), :],
            send_sem=kv_send.at[k], recv_sem=kv_recv.at[k],
            device_id={"band": (up, down)[k], "mp": m}, device_id_type=MESH,
        )

    for k in range(2):
        kv_copy(k).start()
    local[7].wait()
    query = jnp.dot(node[...], pq[...], preferred_element_type=F32).astype(BF16) * BF16(0.125)
    ring_p.relay_left(True)
    ring_p.relay_right(True)
    for k in range(2):
        kv_copy(k).wait_recv()

    span = NODES + 2 * WIN
    vals[0:span, 0:COLS] = kvp[:, COLS:]
    i = lax.broadcasted_iota(jnp.int32, (NODES, span), 0)
    j = lax.broadcasted_iota(jnp.int32, (NODES, span), 1)
    other = b * NODES - WIN + j
    valid = (jnp.abs(i + WIN - j) <= WIN) & (other >= 0) & (other < bands * NODES)
    result, _ = two_heads(query, kvp[:, 0:COLS], vals[0:span, :], jnp.where(valid, 0.0, NEG))
    heads2[:, at_cols(slot * COLS)] = result

    ring_g.start()
    ring_g.start_partner()
    ring_g.relay_left(True)
    ring_g.relay_right(True)
    ring_g.relay_far(True)
    ring_p.relay_far(True)
    local[4].wait()
    ring_p.from_partner()
    ring_g.from_partner()

    def mixed_block(n, carry):
        at = pl.ds(pl.multiple_of(n * 256, 256), 256)
        out[:, at] = (
            latent[:, at] + jnp.dot(heads2[...], pwo_all[:, at], preferred_element_type=F32)
        ).astype(BF16)
        return carry

    lax.fori_loop(0, 4, mixed_block, 0)

    for ring in (ring_k, ring_v):
        ring.drain(False)
    for ring in (ring_o, ring_p, ring_h, ring_g):
        ring.drain(True)
    to_partner.wait_send()
    for d in range(3):
        q_copy(d).wait_send()
        stat_copy(d).wait_send()
        for xs in range(4):
            part_copy(xs, d).wait_send()
    for k in range(2):
        qr_copy(k).wait_send()
        kv_copy(k).wait_send()

    @pl.when(is_rim)
    def _():
        for one in edge_copies:
            one.wait_send()
        for xx in range(4):
            rim_stat_copy(xx).wait_send()
            for xs in range(4):
                rim_copy(xs, xx).wait_send()


def solution(mesh):
    bands = mesh.shape["band"]

    def step(
        grid_latent, grid_gain, hidden_in, hid_gain, enc_wq, enc_wk, enc_wv, enc_wo,
        enc_edges, enc_counts, proc_gain, proc_wq, proc_wk, proc_wv, proc_wo,
    ):
        counts = enc_counts.reshape(1, NODES)
        hbm = pl.BlockSpec(memory_space=pl.ANY)
        vmem = pl.BlockSpec(memory_space=pltpu.VMEM)
        dma = pltpu.SemaphoreType.DMA
        ring_sems = [dma((3, 4, 2)), dma((2, 4, 2))]
        return pl.pallas_call(
            functools.partial(kernel, bands),
            out_shape=jax.ShapeDtypeStruct((NODES, D), BF16),
            in_specs=[hbm] * 10 + [vmem] * 7,
            out_specs=vmem,
            scratch_shapes=[
                pltpu.VMEM((2 * ROWS, D), BF16),
                pltpu.VMEM((2 * ROWS, D), BF16),
                pltpu.VMEM((NODES, D), BF16),
                pltpu.VMEM((4, D, 2 * COLS), BF16),
                pltpu.VMEM((4, NODES, COLS), BF16),
                pltpu.VMEM((4, NODES, COLS), BF16),
                pltpu.VMEM((2 * ROWS, COLS), BF16),
                pltpu.VMEM((2 * ROWS, 2 * COLS), BF16),
                pltpu.VMEM((NODES, 2 * ROWS), F32),
                pltpu.VMEM((NODES, ROWS), F32),
                pltpu.VMEM((NODES, SLOTS), jnp.int32),
                pltpu.VMEM((1, NODES), jnp.int32),
                pltpu.VMEM((4, NODES, COLS), BF16),
                pltpu.VMEM((NODES, 128), F32),
                pltpu.VMEM((4, NODES, COLS), BF16),
                pltpu.VMEM((NODES, 128), F32),
                pltpu.VMEM((6, 4, OWN, COLS), BF16),
                pltpu.VMEM((6, OWN, 128), F32),
                pltpu.VMEM((NODES, D), BF16),
                pltpu.VMEM((D, D), BF16),
                pltpu.VMEM((D, D), BF16),
                pltpu.VMEM((NODES, D), F32),
                pltpu.VMEM((D, 2 * COLS), BF16),
                pltpu.VMEM((D, COLS), BF16),
                pltpu.VMEM((NODES + 2 * WIN, 2 * COLS), BF16),
                pltpu.VMEM((NODES, D), BF16),
            ]
            + ring_sems * 6
            + [
                dma((8,)),
                dma((2,)),
                dma((2, 2)),
                dma((3,)), dma((4,)),
                dma((2,)), dma((4,)),
                dma((3, 4)), dma((6, 4)),
                dma((3,)), dma((6,)),
                dma((4, 4)), dma((4,)),
                dma((2,)), dma((2,)),
            ],
            compiler_params=pltpu.CompilerParams(
                collective_id=0, has_side_effects=True, vmem_limit_bytes=60 * 1024 * 1024
            ),
        )(
            grid_latent, enc_wk, enc_wv, enc_wo, proc_wk, proc_wv, proc_wq, proc_wo, enc_edges, counts,
            grid_gain.reshape(1, D), hidden_in, hid_gain.reshape(1, D), enc_wq, enc_edges, counts,
            proc_gain.reshape(1, D),
        )

    return jax.shard_map(
        step,
        mesh=mesh,
        in_specs=(
            P(("band", "mp"), None), P(), P("band", None), P(),
            P(None, "mp"), P(None, "mp"), P(None, "mp"), P("mp", None),
            P("band", None), P("band"), P(),
            P(None, "mp"), P(None, "mp"), P(None, "mp"), P("mp", None),
        ),
        out_specs=P("band", None),
        check_vma=False,
    )
```

```python
import functools

import jax
import jax.numpy as jnp
from jax import lax
from jax.experimental import pallas as pl
from jax.experimental.pallas import tpu as pltpu
from jax.sharding import PartitionSpec as P

MESH = pl.DeviceIdType.MESH
EPSILON = 1e-05
NEG = -1e30
F32 = jnp.float32
BF16 = jnp.bfloat16

D = 1024
CHIPS = 4
ROWS = 512
NODES = 256
SLOTS = 32
WIN = 128
COLS = 128
HALF = 64
OWN = NODES // CHIPS
RING = 8


def norm_rows(values, gain):
    values = values.astype(F32)
    center = values - jnp.mean(values, axis=-1, keepdims=True)
    spread = jnp.mean(center * center, axis=-1, keepdims=True)
    return center * lax.rsqrt(spread + EPSILON) * gain


def at_cols(start):
    return pl.ds(pl.multiple_of(start, COLS), COLS)


class Ring:
    def __init__(self, place, send, recv, x, c):
        self.place, self.send, self.recv, self.x, self.c = place, send, recv, x, c
        self.others = [lax.rem(x + d, 4) for d in (3, 1, 2)]

    def copy(self, c, x, kind, device):
        ref = self.place(c, x)
        return pltpu.make_async_remote_copy(
            src_ref=ref, dst_ref=ref, send_sem=self.send.at[kind], recv_sem=self.recv.at[c, x],
            device_id={"mp": device}, device_id_type=MESH,
        )

    def sends(self):
        return [self.copy(self.c, self.x, k, 2 * xx + self.c) for k, xx in enumerate(self.others)]

    def to_partner(self, k):
        xx = self.x if k == 3 else self.others[k]
        return self.copy(self.c, xx, 3 + k, 2 * self.x + 1 - self.c)

    def start(self):
        for one in self.sends():
            one.start()
        self.to_partner(3).start()

    def relay(self):
        for k, xx in enumerate(self.others):
            self.copy(self.c, xx, k, 2 * xx + self.c).wait_recv()
            self.to_partner(k).start()

    def from_partner(self):
        for xx in range(4):
            self.copy(1 - self.c, xx, 0, 2 * self.x + 1 - self.c).wait_recv()

    def drain(self):
        for one in self.sends():
            one.wait_send()
        for k in range(4):
            self.to_partner(k).wait_send()


class Spread:
    def __init__(self, source, held, n, index, band_of, x, c, m, sems):
        self.source, self.held, self.n, self.index, self.band_of = source, held, n, index, band_of
        self.x, self.c, self.m = x, c, m
        self.x_send, self.x_recv, self.r_send, self.r_recv, self.p_sem = sems
        self.others = [lax.rem(x + d, 4) for d in (3, 1, 2)]
        self.rows = COLS // n

    def at(self, i):
        return pl.ds(pl.multiple_of(i * self.rows, self.rows), self.rows)

    def over_x(self, k):
        return pltpu.make_async_remote_copy(
            src_ref=self.source.at[self.at(self.index), :],
            dst_ref=self.held.at[self.c * 4 + self.x, self.at(self.index), :],
            send_sem=self.x_send.at[k], recv_sem=self.x_recv.at[self.x],
            device_id={"mp": 2 * self.others[k] + self.c}, device_id_type=MESH,
        )

    def piece(self, k, i, sem, recv, band):
        ref = self.held.at[self.c * 4 + self.others[k], self.at(i), :]
        return pltpu.make_async_remote_copy(
            src_ref=ref, dst_ref=ref, send_sem=sem, recv_sem=recv,
            device_id={"band": band, "mp": self.m}, device_id_type=MESH,
        )

    def along(self, k, d):
        i = lax.rem(self.index + d, self.n)
        return self.piece(
            k, self.index, self.r_send.at[k, d], self.r_recv.at[self.others[k], self.index], self.band_of(i)
        )

    def start(self):
        for k in range(3):
            self.over_x(k).start()

    def spread(self):
        for k in range(3):
            self.piece(
                k, self.index, self.r_send.at[k, 0], self.x_recv.at[self.others[k]], self.band_of(self.index)
            ).wait_recv()
        for d in range(1, self.n):
            for k in range(3):
                self.along(k, d).start()

    def to_partner(self, c):
        ref = self.held.at[pl.ds(c * 4, 4)]
        return pltpu.make_async_remote_copy(
            src_ref=ref, dst_ref=ref, send_sem=self.p_sem.at[0], recv_sem=self.p_sem.at[1],
            device_id={"mp": 2 * self.x + 1 - self.c}, device_id_type=MESH,
        )

    def collect(self):
        for k in range(3):
            for d in range(1, self.n):
                i = lax.rem(self.index + d, self.n)
                self.piece(
                    k, i, self.r_send.at[k, 0], self.r_recv.at[self.others[k], i], self.band_of(i)
                ).wait_recv()
        self.to_partner(self.c).start()

    def from_partner(self):
        self.to_partner(1 - self.c).wait_recv()

    def drain(self):
        for k in range(3):
            self.over_x(k).wait_send()
            for d in range(1, self.n):
                self.along(k, d).wait_send()
        self.to_partner(self.c).wait_send()


def sort_edges(edges_ref, counts_ref, columns_ref, base):
    slot = lax.broadcasted_iota(jnp.int32, (SLOTS, NODES), 0)
    live = jnp.where(slot < counts_ref[...], edges_ref[...] - base, -1).astype(F32)
    columns_ref[...] = jnp.concatenate([live, jnp.full((COLS - SLOTS, NODES), -1.0, F32)], axis=0).T


def fill_bias(columns_ref, bias_ref, width, begin, end):
    step = 16
    column = lax.broadcasted_iota(jnp.int32, (step, width), 1).astype(F32)

    def block(i, carry):
        at = pl.multiple_of(i * step, step)
        edges = columns_ref[pl.ds(at, step), :]
        total = jnp.zeros((step, width), F32)
        for s in range(SLOTS):
            total = total + jnp.where(edges[:, s : s + 1] == column, 1.0, 0.0)
        bias_ref[pl.ds(at, step), :] = jnp.where(
            total > 0.0, jnp.log(jnp.maximum(total, 1.0)), NEG
        )
        return carry

    lax.fori_loop(begin // step, end // step, block, 0)


def two_heads(query, keys, values, bias):
    first = lax.broadcasted_iota(jnp.int32, query.shape, 1) < HALF
    outs, sums = [], []
    for h in range(2):
        q = jnp.where(first if h == 0 else jnp.logical_not(first), query, jnp.zeros_like(query))
        scores = lax.dot_general(q, keys, (((1,), (1,)), ((), ())), preferred_element_type=F32) + bias
        top = jnp.max(scores, axis=1, keepdims=True)
        weights = jnp.exp(scores - top).astype(BF16)
        both = jnp.dot(weights, values, preferred_element_type=F32)
        total = both[:, COLS:]
        outs.append(both[:, :COLS] / total)
        sums.append(top + jnp.log(total))
    return jnp.where(first, outs[0], outs[1]).astype(BF16), sums


def kernel(
    bands, ring,
    grid, wk, wv, wo, pwk, pwv, pwq, pwo, edges_hbm, counts_hbm,
    grid_gain, hidden, hid_gain, wq, edges, counts, proc_gain,
    out,
    raw, normed, node, w, q, qr, keys, vals, bias, bias_r, edges_r, counts_r, columns,
    part, stat, part_r, stat_r, po, st, heads, wo_all, pwo_all, latent, pw, pq, kvp, heads2,
    wx_send, wx_recv, wy_send, wy_recv,
    o0, o1, o2, o3, o4, p0, p1, p2, p3, p4, hs, hr, gs, gr,
    loc, grid_sem, edge_sem, q_send, q_recv, qr_send, qr_recv,
    po_send, po_recv, st_send, st_recv, ro_send, rs_send, kv_send, kv_recv,
):
    b, m = lax.axis_index("band"), lax.axis_index("mp")
    x, c = lax.div(m, 2), lax.rem(m, 2)
    up, down = lax.rem(b + 1, bands), lax.rem(b + bands - 1, bands)
    is_top, is_low = x == 3, x == 0
    is_rim = jnp.logical_or(is_top, is_low)

    layers = bands // ring
    y, z = lax.rem(b, ring), lax.div(b, ring)
    parity = lax.rem(y, 2)

    def band_in_y(i):
        return z * ring + i

    def band_in_z(i):
        return i * ring + y

    ahead, behind = band_in_y(lax.rem(y + 1, ring)), band_in_y(lax.rem(y + ring - 1, ring))

    barrier = pltpu.get_barrier_semaphore()

    def greet(device):
        pl.semaphore_signal(barrier, inc=1, device_id=device, device_id_type=MESH)

    for d in range(1, 8):
        greet({"mp": lax.rem(m + d, 8)})
    for band in (up, down):
        for d in range(4):
            greet({"band": band, "mp": 2 * d + c})
    for d in range(1, ring):
        greet({"band": band_in_y(lax.rem(y + d, ring)), "mp": m})
    for d in range(1, layers):
        greet({"band": band_in_z(lax.rem(z + d, layers)), "mp": m})

    slot = c * 4 + x
    local = [
        pltpu.make_async_copy(wk, w.at[x, :, 0:COLS], loc.at[0]),
        pltpu.make_async_copy(wv, w.at[x, :, COLS:], loc.at[1]),
        pltpu.make_async_copy(grid, raw.at[pl.ds(pl.multiple_of(c * ROWS, ROWS), ROWS), :], loc.at[2]),
        pltpu.make_async_copy(wo, wo_all.at[slot], loc.at[3]),
        pltpu.make_async_copy(pwo, pwo_all.at[slot], loc.at[4]),
        pltpu.make_async_copy(pwk, pw.at[:, 0:COLS], loc.at[5]),
        pltpu.make_async_copy(pwv, pw.at[:, COLS:], loc.at[6]),
        pltpu.make_async_copy(pwq, pq, loc.at[7]),
    ]
    for one in local:
        one.start()
    pl.semaphore_wait(barrier, 13 + ring + layers)

    others = [lax.rem(x + d, 4) for d in (3, 1, 2)]

    def weight_part(xx, mat, row, count):
        return w.at[xx, pl.ds(pl.multiple_of(row, 128), count), pl.ds(mat * COLS, COLS)]

    def weight_x(mat, k, s):
        row = parity * 512 + s * 256
        return pltpu.make_async_remote_copy(
            src_ref=(wk, wv)[mat].at[pl.ds(pl.multiple_of(row, 256), 256), :],
            dst_ref=weight_part(x, mat, row, 256),
            send_sem=wx_send.at[mat, k, s], recv_sem=wx_recv.at[mat, x, s],
            device_id={"mp": 2 * others[k] + c}, device_id_type=MESH,
        )

    def weight_y(mat, k, s, t, half):
        ref = weight_part(others[k], mat, half * 512 + s * 256 + t * 128, 128)
        return pltpu.make_async_remote_copy(
            src_ref=ref, dst_ref=ref,
            send_sem=wy_send.at[mat, k, s, t], recv_sem=wy_recv.at[mat, others[k], s, t],
            device_id={"band": (ahead, behind)[t], "mp": m}, device_id_type=MESH,
        )

    def weight_relay(k, s):
        for mat in range(2):
            ref = weight_part(others[k], mat, parity * 512 + s * 256, 256)
            pltpu.make_async_remote_copy(
                src_ref=ref, dst_ref=ref,
                send_sem=wx_send.at[mat, k, s], recv_sem=wx_recv.at[mat, others[k], s],
                device_id={"mp": 2 * others[k] + c}, device_id_type=MESH,
            ).wait_recv()
            for t in range(2):
                weight_y(mat, k, s, t, parity).start()

    def weight_wait(k):
        for mat in range(2):
            for s in range(2):
                for t in range(2):
                    weight_y(mat, k, s, t, 1 - parity).wait_recv()

    spread_o = Spread(wo, wo_all, layers, z, band_in_z, x, c, m, (o0, o1, o2, o3, o4))
    spread_p = Spread(pwo, pwo_all, ring, y, band_in_y, x, c, m, (p0, p1, p2, p3, p4))

    def head_piece(cc, xx):
        return heads.at[
            pl.ds(pl.multiple_of(xx * OWN, OWN), OWN), pl.ds(pl.multiple_of(cc * 512, 512), 512)
        ]

    def out_piece(cc, xx):
        return heads2.at[:, at_cols((cc * 4 + xx) * COLS)]

    ring_h = Ring(head_piece, hs, hr, x, c)
    ring_g = Ring(out_piece, gs, gr, x, c)

    for mat in range(2):
        for k in range(2):
            weight_x(mat, k, 0).start()
    spread_o.start()
    for k, s in ((0, 1), (1, 1), (2, 0), (2, 1)):
        for mat in range(2):
            weight_x(mat, k, s).start()
    grid_own = pl.ds(pl.multiple_of(c * ROWS, ROWS), ROWS)
    grid_other = pl.ds(pl.multiple_of((1 - c) * ROWS, ROWS), ROWS)
    to_partner = pltpu.make_async_remote_copy(
        src_ref=grid, dst_ref=raw.at[grid_own, :], send_sem=grid_sem.at[0], recv_sem=grid_sem.at[1],
        device_id={"mp": 2 * x + 1 - c}, device_id_type=MESH,
    )
    to_partner.start()

    def rim_input(source, target, k, band):
        return pltpu.make_async_remote_copy(
            src_ref=source, dst_ref=target, send_sem=edge_sem.at[0, k], recv_sem=edge_sem.at[1, k],
            device_id={"band": band, "mp": m}, device_id_type=MESH,
        )

    rim_from = jnp.where(is_top, down, up)
    rim_to = jnp.where(is_top, up, down)
    edge_copies = [
        rim_input(edges_hbm, edges_r, 0, rim_from),
        rim_input(counts_hbm, counts_r, 1, rim_from),
    ]

    @pl.when(is_rim)
    def _():
        for one in edge_copies:
            one.start()

    def node_block(i, carry):
        at = pl.ds(pl.multiple_of(i * 64, 64), 64)
        node[at, :] = norm_rows(hidden[at, :], hid_gain[...]).astype(BF16)
        return carry

    lax.fori_loop(0, NODES // 64, node_block, 0)
    q[x] = jnp.dot(node[...], wq[...], preferred_element_type=F32).astype(BF16) * BF16(0.125)

    def q_copy(d):
        return pltpu.make_async_remote_copy(
            src_ref=q.at[x], dst_ref=q.at[x], send_sem=q_send.at[d], recv_sem=q_recv.at[x],
            device_id={"mp": 2 * lax.rem(x + d + 1, 4) + c}, device_id_type=MESH,
        )

    def qr_copy(k):
        return pltpu.make_async_remote_copy(
            src_ref=q.at[x], dst_ref=qr.at[x], send_sem=qr_send.at[k], recv_sem=qr_recv.at[x],
            device_id={"band": (down, up)[k], "mp": (6, 0)[k] + c}, device_id_type=MESH,
        )

    def q_arrival(ref, sems, xx):
        return pltpu.make_async_remote_copy(
            src_ref=ref.at[xx], dst_ref=ref.at[xx], send_sem=q_send.at[0], recv_sem=sems.at[xx],
            device_id={"mp": 2 * xx + c}, device_id_type=MESH,
        )

    for d in range(3):
        q_copy(d).start()
    for k in range(2):
        qr_copy(k).start()

    def grid_block(i, carry):
        at = pl.ds(pl.multiple_of(i * 64, 64), 64)
        normed[at, :] = norm_rows(raw[at, :], grid_gain[...]).astype(BF16)
        return carry

    base = b * (8 * ROWS) + x * (2 * ROWS)
    rim_row = jnp.where(is_top, ROWS, 0)
    local[2].wait()
    lax.fori_loop(c * 8, c * 8 + 8, grid_block, 0)
    weight_relay(0, 0)
    weight_relay(1, 0)
    sort_edges(edges, counts, columns, base)
    fill_bias(columns, bias, 2 * ROWS, 0, NODES // 2)
    spread_o.spread()
    weight_relay(0, 1)
    weight_relay(1, 1)
    spread_p.start()
    fill_bias(columns, bias, 2 * ROWS, NODES // 2, NODES)
    weight_relay(2, 0)
    vals[:, COLS:] = jnp.ones((2 * ROWS, COLS), BF16)
    stat[...] = jnp.zeros_like(stat)
    stat_r[...] = jnp.zeros_like(stat_r)

    pltpu.make_async_remote_copy(
        src_ref=grid, dst_ref=raw.at[grid_other, :], send_sem=grid_sem.at[0], recv_sem=grid_sem.at[1],
        device_id={"mp": 2 * x + 1 - c}, device_id_type=MESH,
    ).wait_recv()
    lax.fori_loop((1 - c) * 8, (1 - c) * 8 + 8, grid_block, 0)
    weight_relay(2, 1)

    @pl.when(is_rim)
    def _():
        for one in edge_copies:
            one.wait_recv()
        sort_edges(edges_r, counts_r, columns, base + rim_row)
        fill_bias(columns, bias_r, ROWS, 0, NODES)

    spread_p.spread()

    def part_copy(xs, d):
        xx = lax.rem(x + d + 1, 4)
        return pltpu.make_async_remote_copy(
            src_ref=part.at[xs, pl.ds(pl.multiple_of(xx * OWN, OWN), OWN), :],
            dst_ref=po.at[x, xs],
            send_sem=po_send.at[d, xs], recv_sem=po_recv.at[x, xs],
            device_id={"mp": 2 * xx + c}, device_id_type=MESH,
        )

    rim_slot = jnp.where(is_top, 4, 5)

    def rim_copy(xs, xx):
        return pltpu.make_async_remote_copy(
            src_ref=part_r.at[xs, pl.ds(xx * OWN, OWN), :],
            dst_ref=po.at[rim_slot, xs],
            send_sem=ro_send.at[xx, xs], recv_sem=po_recv.at[rim_slot, xs],
            device_id={"band": rim_to, "mp": 2 * xx + c}, device_id_type=MESH,
        )

    def stat_copy(d):
        xx = lax.rem(x + d + 1, 4)
        return pltpu.make_async_remote_copy(
            src_ref=stat.at[pl.ds(pl.multiple_of(xx * OWN, OWN), OWN), :],
            dst_ref=st.at[x],
            send_sem=st_send.at[d], recv_sem=st_recv.at[x],
            device_id={"mp": 2 * xx + c}, device_id_type=MESH,
        )

    def rim_stat_copy(xx):
        return pltpu.make_async_remote_copy(
            src_ref=stat_r.at[pl.ds(xx * OWN, OWN), :],
            dst_ref=st.at[rim_slot],
            send_sem=rs_send.at[xx], recv_sem=st_recv.at[rim_slot],
            device_id={"band": rim_to, "mp": 2 * xx + c}, device_id_type=MESH,
        )

    chunk = 128

    def attend(xs, q_ref, bias_ref, part_ref, stat_ref, first_row, width):
        def block(i, carry):
            at = pl.ds(pl.multiple_of(i * chunk, chunk), chunk)
            span = pl.ds(pl.multiple_of(first_row, ROWS), width)
            result, sums = two_heads(q_ref[xs, at, :], keys[span, :], vals[span, :], bias_ref[at, :])
            part_ref[xs, at, :] = result
            lane = lax.broadcasted_iota(jnp.int32, (chunk, 128), 1)
            old = stat_ref[at, :]
            old = jnp.where(lane == 2 * xs, sums[0], old)
            stat_ref[at, :] = jnp.where(lane == 2 * xs + 1, sums[1], old)
            return carry

        lax.fori_loop(0, NODES // chunk, block, 0)

    def head_step(j, carry):
        xs = lax.rem(x + jnp.where(j == 0, 0, jnp.where(j == 1, 3, jnp.where(j == 2, 1, 2))), 4)

        @pl.when(j == 0)
        def _():
            local[0].wait()
            local[1].wait()

        for k in range(3):

            @pl.when(j == k + 1)
            def _():
                weight_wait(k)

        @pl.when(j > 0)
        def _():
            q_arrival(q, q_recv, xs).wait_recv()

        def project(i, inner):
            at = pl.ds(pl.multiple_of(i * ROWS, ROWS), ROWS)
            both = jnp.dot(normed[at, :], w[xs], preferred_element_type=F32).astype(BF16)
            keys[at, :] = both[:, :COLS]
            vals[at, 0:COLS] = both[:, COLS:]
            return inner

        lax.fori_loop(0, 2, project, 0)

        @pl.when(is_rim)
        def _():
            q_arrival(qr, qr_recv, xs).wait_recv()
            attend(xs, qr, bias_r, part_r, stat_r, rim_row, ROWS)
            for xx in range(4):
                rim_copy(xs, xx).start()

        attend(xs, q, bias, part, stat, 0, 2 * ROWS)
        for d in range(3):
            part_copy(xs, d).start()
        return carry

    lax.fori_loop(0, 4, head_step, 0)

    for d in range(3):
        stat_copy(d).start()

    @pl.when(is_rim)
    def _():
        for xx in range(4):
            rim_stat_copy(xx).start()

    mine = pl.ds(pl.multiple_of(x * OWN, OWN), OWN)
    st[x] = stat[mine, :]
    for xs in range(4):
        po[x, xs] = part[xs, mine, :]

    def arrivals(i):
        for xs in range(4):
            pltpu.make_async_remote_copy(
                src_ref=po.at[i, xs], dst_ref=po.at[i, xs],
                send_sem=po_send.at[0, xs], recv_sem=po_recv.at[i, xs],
                device_id={"mp": m}, device_id_type=MESH,
            ).wait_recv()
        pltpu.make_async_remote_copy(
            src_ref=st.at[i], dst_ref=st.at[i], send_sem=st_send.at[0], recv_sem=st_recv.at[i],
            device_id={"mp": m}, device_id_type=MESH,
        ).wait_recv()

    for d in range(3):
        arrivals(lax.rem(x + d + 1, 4))
    arrivals(4)
    arrivals(5)

    top = st[0]
    for i in range(1, 6):
        top = jnp.maximum(top, st[i])
    shares = [jnp.exp(st[i] - top) for i in range(6)]
    whole = shares[0]
    for i in range(1, 6):
        whole = whole + shares[i]
    shares = [one / whole for one in shares]
    first = lax.broadcasted_iota(jnp.int32, (OWN, COLS), 1) < HALF
    for xs in range(4):
        total = jnp.zeros((OWN, COLS), F32)
        for i in range(6):
            left = jnp.broadcast_to(shares[i][:, 2 * xs : 2 * xs + 1], (OWN, COLS))
            right = jnp.broadcast_to(shares[i][:, 2 * xs + 1 : 2 * xs + 2], (OWN, COLS))
            total = total + jnp.where(first, left, right) * po[i, xs].astype(F32)
        heads[mine, at_cols(c * 512 + xs * COLS)] = total.astype(BF16)

    ring_h.start()
    ring_h.relay()
    local[3].wait()
    spread_o.collect()

    def half_product(left, right, cc, at):
        return jnp.dot(
            left[:, pl.ds(pl.multiple_of(cc * 512, 512), 512)],
            right[pl.ds(cc * 4, 4), :, at].reshape(512, 256),
            preferred_element_type=F32,
        )

    def latent_first(n, carry):
        at = pl.ds(pl.multiple_of(n * 256, 256), 256)
        latent[:, at] = hidden[:, at].astype(F32) + half_product(heads, wo_all, c, at)
        return carry

    def latent_second(n, carry):
        at = pl.ds(pl.multiple_of(n * 256, 256), 256)
        latent[:, at] = latent[:, at] + half_product(heads, wo_all, 1 - c, at)
        return carry

    lax.fori_loop(0, 4, latent_first, 0)
    ring_h.from_partner()
    spread_o.from_partner()
    lax.fori_loop(0, 4, latent_second, 0)

    def latent_norm(i, carry):
        at = pl.ds(pl.multiple_of(i * 64, 64), 64)
        node[at, :] = norm_rows(latent[at, :], proc_gain[...]).astype(BF16)
        return carry

    lax.fori_loop(0, NODES // 64, latent_norm, 0)

    local[5].wait()
    local[6].wait()
    kvp[WIN : WIN + NODES, :] = jnp.dot(
        node[...], pw[...], preferred_element_type=F32
    ).astype(BF16)

    def kv_copy(k):
        source, target = ((NODES, 0), (WIN, WIN + NODES))[k]
        return pltpu.make_async_remote_copy(
            src_ref=kvp.at[pl.ds(source, WIN), :], dst_ref=kvp.at[pl.ds(target, WIN), :],
            send_sem=kv_send.at[k], recv_sem=kv_recv.at[k],
            device_id={"band": (up, down)[k], "mp": m}, device_id_type=MESH,
        )

    for k in range(2):
        kv_copy(k).start()
    local[7].wait()
    query = jnp.dot(node[...], pq[...], preferred_element_type=F32).astype(BF16) * BF16(0.125)
    local[4].wait()
    spread_p.collect()
    for k in range(2):
        kv_copy(k).wait_recv()

    span = NODES + 2 * WIN
    vals[0:span, 0:COLS] = kvp[:, COLS:]
    i = lax.broadcasted_iota(jnp.int32, (NODES, span), 0)
    j = lax.broadcasted_iota(jnp.int32, (NODES, span), 1)
    other = b * NODES - WIN + j
    valid = (jnp.abs(i + WIN - j) <= WIN) & (other >= 0) & (other < bands * NODES)
    result, _ = two_heads(query, kvp[:, 0:COLS], vals[0:span, :], jnp.where(valid, 0.0, NEG))
    heads2[:, at_cols(slot * COLS)] = result

    ring_g.start()
    ring_g.relay()

    def mixed_first(n, carry):
        at = pl.ds(pl.multiple_of(n * 256, 256), 256)
        latent[:, at] = latent[:, at] + half_product(heads2, pwo_all, c, at)
        return carry

    def mixed_second(n, carry):
        at = pl.ds(pl.multiple_of(n * 256, 256), 256)
        out[:, at] = (latent[:, at] + half_product(heads2, pwo_all, 1 - c, at)).astype(BF16)
        return carry

    lax.fori_loop(0, 4, mixed_first, 0)
    ring_g.from_partner()
    spread_p.from_partner()
    lax.fori_loop(0, 4, mixed_second, 0)

    for mat in range(2):
        for k in range(3):
            for s in range(2):
                weight_x(mat, k, s).wait_send()
                for t in range(2):
                    weight_y(mat, k, s, t, parity).wait_send()
    for one in (spread_o, spread_p, ring_h, ring_g):
        one.drain()
    to_partner.wait_send()
    for d in range(3):
        q_copy(d).wait_send()
        stat_copy(d).wait_send()
        for xs in range(4):
            part_copy(xs, d).wait_send()
    for k in range(2):
        qr_copy(k).wait_send()
        kv_copy(k).wait_send()

    @pl.when(is_rim)
    def _():
        for one in edge_copies:
            one.wait_send()
        for xx in range(4):
            rim_stat_copy(xx).wait_send()
            for xs in range(4):
                rim_copy(xs, xx).wait_send()


def solution(mesh):
    bands = mesh.shape["band"]
    ring = RING if bands % RING == 0 else 2
    layers = bands // ring

    def step(
        grid_latent, grid_gain, hidden_in, hid_gain, enc_wq, enc_wk, enc_wv, enc_wo,
        enc_edges, enc_counts, proc_gain, proc_wq, proc_wk, proc_wv, proc_wo,
    ):
        counts = enc_counts.reshape(1, NODES)
        edges = enc_edges.T
        hbm = pl.BlockSpec(memory_space=pl.ANY)
        vmem = pl.BlockSpec(memory_space=pltpu.VMEM)
        dma = pltpu.SemaphoreType.DMA
        spread_sems = lambda n: [dma((3,)), dma((4,)), dma((3, n)), dma((4, n)), dma((2,))]
        ring_sems = [dma((7,)), dma((2, 4))]
        return pl.pallas_call(
            functools.partial(kernel, bands, ring),
            out_shape=jax.ShapeDtypeStruct((NODES, D), BF16),
            in_specs=[hbm] * 10 + [vmem] * 7,
            out_specs=vmem,
            scratch_shapes=[
                pltpu.VMEM((2 * ROWS, D), BF16),
                pltpu.VMEM((2 * ROWS, D), BF16),
                pltpu.VMEM((NODES, D), BF16),
                pltpu.VMEM((4, D, 2 * COLS), BF16),
                pltpu.VMEM((4, NODES, COLS), BF16),
                pltpu.VMEM((4, NODES, COLS), BF16),
                pltpu.VMEM((2 * ROWS, COLS), BF16),
                pltpu.VMEM((2 * ROWS, 2 * COLS), BF16),
                pltpu.VMEM((NODES, 2 * ROWS), F32),
                pltpu.VMEM((NODES, ROWS), F32),
                pltpu.VMEM((SLOTS, NODES), jnp.int32),
                pltpu.VMEM((1, NODES), jnp.int32),
                pltpu.VMEM((NODES, COLS), F32),
                pltpu.VMEM((4, NODES, COLS), BF16),
                pltpu.VMEM((NODES, 128), F32),
                pltpu.VMEM((4, NODES, COLS), BF16),
                pltpu.VMEM((NODES, 128), F32),
                pltpu.VMEM((6, 4, OWN, COLS), BF16),
                pltpu.VMEM((6, OWN, 128), F32),
                pltpu.VMEM((NODES, D), BF16),
                pltpu.VMEM((8, COLS, D), BF16),
                pltpu.VMEM((8, COLS, D), BF16),
                pltpu.VMEM((NODES, D), F32),
                pltpu.VMEM((D, 2 * COLS), BF16),
                pltpu.VMEM((D, COLS), BF16),
                pltpu.VMEM((NODES + 2 * WIN, 2 * COLS), BF16),
                pltpu.VMEM((NODES, D), BF16),
            ]
            + [dma((2, 3, 2)), dma((2, 4, 2)), dma((2, 3, 2, 2)), dma((2, 4, 2, 2))]
            + spread_sems(layers)
            + spread_sems(ring)
            + ring_sems * 2
            + [
                dma((8,)),
                dma((2,)),
                dma((2, 2)),
                dma((3,)), dma((4,)),
                dma((2,)), dma((4,)),
                dma((3, 4)), dma((6, 4)),
                dma((3,)), dma((6,)),
                dma((4, 4)), dma((4,)),
                dma((2,)), dma((2,)),
            ],
            compiler_params=pltpu.CompilerParams(
                collective_id=0, has_side_effects=True, vmem_limit_bytes=60 * 1024 * 1024
            ),
        )(
            grid_latent, enc_wk, enc_wv, enc_wo, proc_wk, proc_wv, proc_wq, proc_wo, edges, counts,
            grid_gain.reshape(1, D), hidden_in, hid_gain.reshape(1, D), enc_wq, edges, counts,
            proc_gain.reshape(1, D),
        )

    return jax.shard_map(
        step,
        mesh=mesh,
        in_specs=(
            P(("band", "mp"), None), P(), P("band", None), P(),
            P(None, "mp"), P(None, "mp"), P(None, "mp"), P("mp", None),
            P("band", None), P("band"), P(),
            P(None, "mp"), P(None, "mp"), P(None, "mp"), P("mp", None),
        ),
        out_specs=P("band", None),
        check_vma=False,
    )
```

```python
import functools

import jax
import jax.numpy as jnp
from jax import lax
from jax.experimental import pallas as pl
from jax.experimental.pallas import tpu as pltpu
from jax.sharding import PartitionSpec as P

MESH = pl.DeviceIdType.MESH
EPSILON = 1e-05
NEG = -1e30
F32 = jnp.float32
BF16 = jnp.bfloat16

D = 1024
CHIPS = 4
ROWS = 512
NODES = 256
SLOTS = 32
WIN = 128
COLS = 128
HALF = 64
OWN = NODES // CHIPS
RING = 8


def norm_rows(values, gain):
    values = values.astype(F32)
    center = values - jnp.mean(values, axis=-1, keepdims=True)
    spread = jnp.mean(center * center, axis=-1, keepdims=True)
    return center * lax.rsqrt(spread + EPSILON) * gain


def at_cols(start):
    return pl.ds(pl.multiple_of(start, COLS), COLS)


class Ring:
    def __init__(self, place, send, recv, x, c):
        self.place, self.send, self.recv, self.x, self.c = place, send, recv, x, c
        self.others = [lax.rem(x + d, 4) for d in (3, 1, 2)]

    def copy(self, c, x, kind, device):
        ref = self.place(c, x)
        return pltpu.make_async_remote_copy(
            src_ref=ref, dst_ref=ref, send_sem=self.send.at[kind], recv_sem=self.recv.at[c, x],
            device_id={"mp": device}, device_id_type=MESH,
        )

    def sends(self):
        return [self.copy(self.c, self.x, k, 2 * xx + self.c) for k, xx in enumerate(self.others)]

    def to_partner(self, k):
        xx = self.x if k == 3 else self.others[k]
        return self.copy(self.c, xx, 3 + k, 2 * self.x + 1 - self.c)

    def start(self):
        for one in self.sends():
            one.start()
        self.to_partner(3).start()

    def relay(self):
        for k, xx in enumerate(self.others):
            self.copy(self.c, xx, k, 2 * xx + self.c).wait_recv()
            self.to_partner(k).start()

    def from_partner(self):
        for xx in range(4):
            self.copy(1 - self.c, xx, 0, 2 * self.x + 1 - self.c).wait_recv()

    def drain(self):
        for one in self.sends():
            one.wait_send()
        for k in range(4):
            self.to_partner(k).wait_send()


class Spread:
    def __init__(self, source, held, n, index, band_of, x, c, m, sems):
        self.source, self.held, self.n, self.index, self.band_of = source, held, n, index, band_of
        self.x, self.c, self.m = x, c, m
        self.x_send, self.x_recv, self.r_send, self.r_recv, self.p_sem = sems
        self.others = [lax.rem(x + d, 4) for d in (3, 1, 2)]
        self.rows = COLS // n

    def at(self, i):
        return pl.ds(pl.multiple_of(i * self.rows, self.rows), self.rows)

    def over_x(self, k):
        return pltpu.make_async_remote_copy(
            src_ref=self.source.at[self.at(self.index), :],
            dst_ref=self.held.at[self.c * 4 + self.x, self.at(self.index), :],
            send_sem=self.x_send.at[k], recv_sem=self.x_recv.at[self.x],
            device_id={"mp": 2 * self.others[k] + self.c}, device_id_type=MESH,
        )

    def piece(self, k, i, sem, recv, band):
        ref = self.held.at[self.c * 4 + self.others[k], self.at(i), :]
        return pltpu.make_async_remote_copy(
            src_ref=ref, dst_ref=ref, send_sem=sem, recv_sem=recv,
            device_id={"band": band, "mp": self.m}, device_id_type=MESH,
        )

    def along(self, k, d):
        i = lax.rem(self.index + d, self.n)
        return self.piece(
            k, self.index, self.r_send.at[k, d], self.r_recv.at[self.others[k], self.index], self.band_of(i)
        )

    def start(self):
        for k in range(3):
            self.over_x(k).start()

    def spread(self):
        for k in range(3):
            self.piece(
                k, self.index, self.r_send.at[k, 0], self.x_recv.at[self.others[k]], self.band_of(self.index)
            ).wait_recv()
        for d in range(1, self.n):
            for k in range(3):
                self.along(k, d).start()

    def to_partner(self, c):
        ref = self.held.at[pl.ds(c * 4, 4)]
        return pltpu.make_async_remote_copy(
            src_ref=ref, dst_ref=ref, send_sem=self.p_sem.at[0], recv_sem=self.p_sem.at[1],
            device_id={"mp": 2 * self.x + 1 - self.c}, device_id_type=MESH,
        )

    def collect(self):
        for k in range(3):
            for d in range(1, self.n):
                i = lax.rem(self.index + d, self.n)
                self.piece(
                    k, i, self.r_send.at[k, 0], self.r_recv.at[self.others[k], i], self.band_of(i)
                ).wait_recv()
        self.to_partner(self.c).start()

    def from_partner(self):
        self.to_partner(1 - self.c).wait_recv()

    def drain(self):
        for k in range(3):
            self.over_x(k).wait_send()
            for d in range(1, self.n):
                self.along(k, d).wait_send()
        self.to_partner(self.c).wait_send()


def code_of(index):
    high = jnp.clip(index >> 7, 0, 7)
    return ((COLS + (index & 127)) << high).astype(F32)


def sort_edges(edges_ref, counts_ref, columns_ref, base, width):
    slot = lax.broadcasted_iota(jnp.int32, (SLOTS, NODES), 0)
    index = edges_ref[...] - base
    live = (slot < counts_ref[...]) & (index >= 0) & (index < width)
    codes = jnp.where(live, code_of(index), -1.0)
    columns_ref[...] = jnp.concatenate([codes, jnp.full((COLS - SLOTS, NODES), -1.0, F32)], axis=0).T.astype(BF16)


def fill_bias(columns_ref, bias_ref, width, begin, end):
    step = 16
    column = code_of(lax.broadcasted_iota(jnp.int32, (step, width), 1)).astype(BF16)

    def block(i, carry):
        at = pl.multiple_of(i * step, step)
        edges = columns_ref[pl.ds(at, step), :]
        total = jnp.zeros((step, width), BF16)
        for s in range(SLOTS):
            total = total + jnp.where(edges[:, s : s + 1] == column, BF16(1), BF16(0))
        total = total.astype(F32)
        bias_ref[pl.ds(at, step), :] = jnp.where(
            total > 0.0, jnp.log(jnp.maximum(total, 1.0)), NEG
        )
        return carry

    lax.fori_loop(begin // step, end // step, block, 0)


def two_heads(query, keys, values, bias):
    first = lax.broadcasted_iota(jnp.int32, query.shape, 1) < HALF
    outs, sums = [], []
    for h in range(2):
        q = jnp.where(first if h == 0 else jnp.logical_not(first), query, jnp.zeros_like(query))
        scores = lax.dot_general(q, keys, (((1,), (1,)), ((), ())), preferred_element_type=F32) + bias
        top = jnp.max(scores, axis=1, keepdims=True)
        weights = jnp.exp(scores - top).astype(BF16)
        both = jnp.dot(weights, values, preferred_element_type=F32)
        total = both[:, COLS:]
        outs.append(both[:, :COLS] / total)
        sums.append(top + jnp.log(total))
    return jnp.where(first, outs[0], outs[1]).astype(BF16), sums


def kernel(
    bands, ring,
    grid, wk, wv, wo, pwk, pwv, pwq, pwo, edges_hbm, counts_hbm,
    grid_gain, hidden, hid_gain, wq, edges, counts, proc_gain,
    out,
    raw, normed, node, w, q, qr, keys, vals, bias, bias_r, edges_r, counts_r, columns,
    part, stat, stat_t, part_r, stat_r, stat_rt, spare, po, st, heads, wo_all, pwo_all, latent, pw, pq, kvp, heads2,
    wx_send, wx_recv, wy_send, wy_recv,
    o0, o1, o2, o3, o4, p0, p1, p2, p3, p4, hs, hr, gs, gr,
    loc, grid_sem, edge_sem, q_send, q_recv, qr_send, qr_recv,
    po_send, po_recv, st_send, st_recv, ro_send, rs_send, kv_send, kv_recv,
):
    b, m = lax.axis_index("band"), lax.axis_index("mp")
    x, c = lax.div(m, 2), lax.rem(m, 2)
    up, down = lax.rem(b + 1, bands), lax.rem(b + bands - 1, bands)
    is_top, is_low = x == 3, x == 0
    is_rim = jnp.logical_or(is_top, is_low)

    layers = bands // ring
    y, z = lax.rem(b, ring), lax.div(b, ring)
    parity = lax.rem(y, 2)

    def band_in_y(i):
        return z * ring + i

    def band_in_z(i):
        return i * ring + y

    ahead, behind = band_in_y(lax.rem(y + 1, ring)), band_in_y(lax.rem(y + ring - 1, ring))

    barrier = pltpu.get_barrier_semaphore()

    def greet(device):
        pl.semaphore_signal(barrier, inc=1, device_id=device, device_id_type=MESH)

    for d in range(1, 8):
        greet({"mp": lax.rem(m + d, 8)})
    for band in (up, down):
        for d in range(4):
            greet({"band": band, "mp": 2 * d + c})
    for d in range(1, ring):
        greet({"band": band_in_y(lax.rem(y + d, ring)), "mp": m})
    for d in range(1, layers):
        greet({"band": band_in_z(lax.rem(z + d, layers)), "mp": m})

    slot = c * 4 + x
    local = [
        pltpu.make_async_copy(wk, w.at[x, :, 0:COLS], loc.at[0]),
        pltpu.make_async_copy(wv, w.at[x, :, COLS:], loc.at[1]),
        pltpu.make_async_copy(grid, raw, loc.at[2]),
        pltpu.make_async_copy(wo, wo_all.at[slot], loc.at[3]),
        pltpu.make_async_copy(pwo, pwo_all.at[slot], loc.at[4]),
        pltpu.make_async_copy(pwk, pw.at[:, 0:COLS], loc.at[5]),
        pltpu.make_async_copy(pwv, pw.at[:, COLS:], loc.at[6]),
        pltpu.make_async_copy(pwq, pq, loc.at[7]),
    ]
    for one in local:
        one.start()
    pl.semaphore_wait(barrier, 13 + ring + layers)

    others = [lax.rem(x + d, 4) for d in (3, 1, 2)]

    def weight_part(xx, mat, row, count):
        return w.at[xx, pl.ds(pl.multiple_of(row, 128), count), pl.ds(mat * COLS, COLS)]

    def weight_x(mat, k, s):
        row = parity * 512 + s * 256
        return pltpu.make_async_remote_copy(
            src_ref=(wk, wv)[mat].at[pl.ds(pl.multiple_of(row, 256), 256), :],
            dst_ref=weight_part(x, mat, row, 256),
            send_sem=wx_send.at[mat, k, s], recv_sem=wx_recv.at[mat, x, s],
            device_id={"mp": 2 * others[k] + c}, device_id_type=MESH,
        )

    def weight_y(mat, k, s, t, half):
        ref = weight_part(others[k], mat, half * 512 + s * 256 + t * 128, 128)
        return pltpu.make_async_remote_copy(
            src_ref=ref, dst_ref=ref,
            send_sem=wy_send.at[mat, k, s, t], recv_sem=wy_recv.at[mat, others[k], s, t],
            device_id={"band": (ahead, behind)[t], "mp": m}, device_id_type=MESH,
        )

    def weight_relay(k, s):
        for mat in range(2):
            ref = weight_part(others[k], mat, parity * 512 + s * 256, 256)
            pltpu.make_async_remote_copy(
                src_ref=ref, dst_ref=ref,
                send_sem=wx_send.at[mat, k, s], recv_sem=wx_recv.at[mat, others[k], s],
                device_id={"mp": 2 * others[k] + c}, device_id_type=MESH,
            ).wait_recv()
            for t in range(2):
                weight_y(mat, k, s, t, parity).start()

    def weight_wait(k):
        for mat in range(2):
            for s in range(2):
                for t in range(2):
                    weight_y(mat, k, s, t, 1 - parity).wait_recv()

    spread_o = Spread(wo, wo_all, layers, z, band_in_z, x, c, m, (o0, o1, o2, o3, o4))
    spread_p = Spread(pwo, pwo_all, layers, z, band_in_z, x, c, m, (p0, p1, p2, p3, p4))

    def head_piece(cc, xx):
        return heads.at[
            pl.ds(pl.multiple_of(xx * OWN, OWN), OWN), pl.ds(pl.multiple_of(cc * 512, 512), 512)
        ]

    def out_piece(cc, xx):
        return heads2.at[:, at_cols((cc * 4 + xx) * COLS)]

    ring_h = Ring(head_piece, hs, hr, x, c)
    ring_g = Ring(out_piece, gs, gr, x, c)

    for mat in range(2):
        for k in range(2):
            weight_x(mat, k, 0).start()
    spread_o.start()
    for mat in range(2):
        for k in range(2):
            weight_x(mat, k, 1).start()
    grid_own = pl.ds(pl.multiple_of(c * ROWS, ROWS), ROWS)
    grid_other = pl.ds(pl.multiple_of((1 - c) * ROWS, ROWS), ROWS)

    def rows_to_partner(at):
        return pltpu.make_async_remote_copy(
            src_ref=normed.at[at, :], dst_ref=normed.at[at, :], send_sem=grid_sem.at[0], recv_sem=grid_sem.at[1],
            device_id={"mp": 2 * x + 1 - c}, device_id_type=MESH,
        )

    def rim_input(source, target, k, band):
        return pltpu.make_async_remote_copy(
            src_ref=source, dst_ref=target, send_sem=edge_sem.at[0, k], recv_sem=edge_sem.at[1, k],
            device_id={"band": band, "mp": m}, device_id_type=MESH,
        )

    rim_from = jnp.where(is_top, down, up)
    rim_to = jnp.where(is_top, up, down)
    edge_copies = [
        rim_input(edges_hbm, edges_r, 0, rim_from),
        rim_input(counts_hbm, counts_r, 1, rim_from),
    ]

    @pl.when(is_rim)
    def _():
        for one in edge_copies:
            one.start()

    def node_block(i, carry):
        at = pl.ds(pl.multiple_of(i * 64, 64), 64)
        node[at, :] = norm_rows(hidden[at, :], hid_gain[...]).astype(BF16)
        return carry

    lax.fori_loop(0, NODES // 64, node_block, 0)
    q[x] = jnp.dot(node[...], wq[...], preferred_element_type=F32).astype(BF16) * BF16(0.125)

    def q_copy(d):
        return pltpu.make_async_remote_copy(
            src_ref=q.at[x], dst_ref=q.at[x], send_sem=q_send.at[d], recv_sem=q_recv.at[x],
            device_id={"mp": 2 * lax.rem(x + d + 1, 4) + c}, device_id_type=MESH,
        )

    def qr_copy(k):
        return pltpu.make_async_remote_copy(
            src_ref=q.at[x], dst_ref=qr.at[x], send_sem=qr_send.at[k], recv_sem=qr_recv.at[x],
            device_id={"band": (down, up)[k], "mp": (6, 0)[k] + c}, device_id_type=MESH,
        )

    def q_arrival(ref, sems, xx):
        return pltpu.make_async_remote_copy(
            src_ref=ref.at[xx], dst_ref=ref.at[xx], send_sem=q_send.at[0], recv_sem=sems.at[xx],
            device_id={"mp": 2 * xx + c}, device_id_type=MESH,
        )

    for d in range(3):
        q_copy(d).start()
    for k in range(2):
        qr_copy(k).start()
    for mat in range(2):
        for s in range(2):
            weight_x(mat, 2, s).start()
    spread_p.start()

    def grid_block(i, carry):
        at = pl.ds(pl.multiple_of(i * 64, 64), 64)
        normed[pl.ds(pl.multiple_of(c * ROWS + i * 64, 64), 64), :] = norm_rows(raw[at, :], grid_gain[...]).astype(BF16)
        return carry

    base = b * (8 * ROWS) + x * (2 * ROWS)
    rim_row = jnp.where(is_top, ROWS, 0)
    local[2].wait()
    lax.fori_loop(0, ROWS // 64, grid_block, 0)
    rows_to_partner(grid_own).start()
    sort_edges(edges, counts, columns, base, 2 * ROWS)
    fill_bias(columns, bias, 2 * ROWS, 0, NODES // 2)
    weight_relay(0, 0)
    weight_relay(1, 0)
    fill_bias(columns, bias, 2 * ROWS, NODES // 2, NODES)
    spread_o.spread()
    weight_relay(0, 1)
    weight_relay(1, 1)
    vals[:, COLS:] = jnp.ones((2 * ROWS, COLS), BF16)
    stat[...] = jnp.zeros_like(stat)
    stat_r[...] = jnp.zeros_like(stat_r)

    @pl.when(is_rim)
    def _():
        for one in edge_copies:
            one.wait_recv()
        sort_edges(edges_r, counts_r, columns, base + rim_row, ROWS)
        fill_bias(columns, bias_r, ROWS, 0, NODES)

    rows_to_partner(grid_other).wait_recv()

    def part_copy(xs, d):
        xx = lax.rem(x + d + 1, 4)
        return pltpu.make_async_remote_copy(
            src_ref=part.at[xs, pl.ds(pl.multiple_of(xx * OWN, OWN), OWN), :],
            dst_ref=po.at[x, xs],
            send_sem=po_send.at[d, xs], recv_sem=po_recv.at[x, xs],
            device_id={"mp": 2 * xx + c}, device_id_type=MESH,
        )

    rim_slot = jnp.where(is_top, 4, 5)

    def rim_copy(xs, xx):
        return pltpu.make_async_remote_copy(
            src_ref=part_r.at[xs, pl.ds(xx * OWN, OWN), :],
            dst_ref=po.at[rim_slot, xs],
            send_sem=ro_send.at[xx, xs], recv_sem=po_recv.at[rim_slot, xs],
            device_id={"band": rim_to, "mp": 2 * xx + c}, device_id_type=MESH,
        )

    def stat_copy(d):
        xx = lax.rem(x + d + 1, 4)
        return pltpu.make_async_remote_copy(
            src_ref=stat_t.at[lax.div(xx, 2)], dst_ref=st.at[x],
            send_sem=st_send.at[d], recv_sem=st_recv.at[x],
            device_id={"mp": 2 * xx + c}, device_id_type=MESH,
        )

    def rim_stat_copy(xx):
        return pltpu.make_async_remote_copy(
            src_ref=stat_rt.at[xx // 2], dst_ref=st.at[rim_slot],
            send_sem=rs_send.at[xx], recv_sem=st_recv.at[rim_slot],
            device_id={"band": rim_to, "mp": 2 * xx + c}, device_id_type=MESH,
        )

    chunk = 128

    def attend(xs, q_ref, bias_ref, part_ref, stat_ref, first_row, width):
        def block(i, carry):
            at = pl.ds(pl.multiple_of(i * chunk, chunk), chunk)
            span = pl.ds(pl.multiple_of(first_row, ROWS), width)
            result, sums = two_heads(q_ref[xs, at, :], keys[span, :], vals[span, :], bias_ref[at, :])
            part_ref[xs, at, :] = result
            lane = lax.broadcasted_iota(jnp.int32, (chunk, 128), 1)
            old = stat_ref[at, :]
            old = jnp.where(lane == 2 * xs, sums[0], old)
            stat_ref[at, :] = jnp.where(lane == 2 * xs + 1, sums[1], old)
            return carry

        lax.fori_loop(0, NODES // chunk, block, 0)

    def slice_of(xs):
        def project(i, inner):
            at = pl.ds(pl.multiple_of(i * ROWS, ROWS), ROWS)
            both = jnp.dot(normed[at, :], w[xs], preferred_element_type=F32).astype(BF16)
            keys[at, :] = both[:, :COLS]
            vals[at, 0:COLS] = both[:, COLS:]
            return inner

        lax.fori_loop(0, 2, project, 0)

        @pl.when(is_rim)
        def _():
            q_arrival(qr, qr_recv, xs).wait_recv()
            attend(xs, qr, bias_r, part_r, stat_r, rim_row, ROWS)
            for xx in range(4):
                rim_copy(xs, xx).start()

        attend(xs, q, bias, part, stat, 0, 2 * ROWS)
        for d in range(3):
            part_copy(xs, d).start()

    def head_step(j, carry):
        xs = lax.rem(x + jnp.where(j == 1, 3, jnp.where(j == 2, 1, 2)), 4)
        for k in range(3):

            @pl.when(j == k + 1)
            def _():
                weight_wait(k)

        q_arrival(q, q_recv, xs).wait_recv()
        slice_of(xs)
        return carry

    local[0].wait()
    local[1].wait()
    slice_of(x)
    weight_relay(2, 0)
    weight_relay(2, 1)
    spread_p.spread()
    lax.fori_loop(1, 4, head_step, 0)

    for half in range(2):
        stat_t[half] = stat[half * 128 : half * 128 + 128, :].T[0:8]
    for d in range(3):
        stat_copy(d).start()

    @pl.when(is_rim)
    def _():
        for half in range(2):
            stat_rt[half] = stat_r[half * 128 : half * 128 + 128, :].T[0:8]
        for xx in range(4):
            rim_stat_copy(xx).start()

    mine = pl.ds(pl.multiple_of(x * OWN, OWN), OWN)
    st[x] = stat_t[lax.div(x, 2)]
    for xs in range(4):
        po[x, xs] = part[xs, mine, :]

    def arrivals(i):
        for xs in range(4):
            pltpu.make_async_remote_copy(
                src_ref=po.at[i, xs], dst_ref=po.at[i, xs],
                send_sem=po_send.at[0, xs], recv_sem=po_recv.at[i, xs],
                device_id={"mp": m}, device_id_type=MESH,
            ).wait_recv()
        pltpu.make_async_remote_copy(
            src_ref=st.at[i], dst_ref=st.at[i], send_sem=st_send.at[0], recv_sem=st_recv.at[i],
            device_id={"mp": m}, device_id_type=MESH,
        ).wait_recv()

    for d in range(3):
        arrivals(lax.rem(x + d + 1, 4))
    arrivals(4)
    arrivals(5)

    top = st[0]
    for i in range(1, 6):
        top = jnp.maximum(top, st[i])
    shares = [jnp.exp(st[i] - top) for i in range(6)]
    whole = shares[0]
    for i in range(1, 6):
        whole = whole + shares[i]
    shares = [one / whole for one in shares]
    spare[...] = jnp.concatenate(shares + [jnp.zeros((128 - 48, 128), F32)], axis=0).T
    share = spare[pl.ds(pl.multiple_of(lax.rem(x, 2) * OWN, OWN), OWN), :]
    first = lax.broadcasted_iota(jnp.int32, (OWN, COLS), 1) < HALF
    for xs in range(4):
        total = jnp.zeros((OWN, COLS), F32)
        for i in range(6):
            at = i * 8 + 2 * xs
            left = jnp.broadcast_to(share[:, at : at + 1], (OWN, COLS))
            right = jnp.broadcast_to(share[:, at + 1 : at + 2], (OWN, COLS))
            total = total + jnp.where(first, left, right) * po[i, xs].astype(F32)
        heads[mine, at_cols(c * 512 + xs * COLS)] = total.astype(BF16)

    ring_h.start()
    ring_h.relay()
    local[3].wait()
    spread_o.collect()

    def half_product(left, right, cc, at):
        return jnp.dot(
            left[:, pl.ds(pl.multiple_of(cc * 512, 512), 512)],
            right[pl.ds(cc * 4, 4), :, at].reshape(512, 256),
            preferred_element_type=F32,
        )

    def latent_first(n, carry):
        at = pl.ds(pl.multiple_of(n * 256, 256), 256)
        latent[:, at] = hidden[:, at].astype(F32) + half_product(heads, wo_all, c, at)
        return carry

    def latent_second(n, carry):
        at = pl.ds(pl.multiple_of(n * 256, 256), 256)
        latent[:, at] = latent[:, at] + half_product(heads, wo_all, 1 - c, at)
        return carry

    lax.fori_loop(0, 4, latent_first, 0)
    ring_h.from_partner()
    spread_o.from_partner()
    lax.fori_loop(0, 4, latent_second, 0)

    def latent_norm(i, carry):
        at = pl.ds(pl.multiple_of(i * 64, 64), 64)
        node[at, :] = norm_rows(latent[at, :], proc_gain[...]).astype(BF16)
        return carry

    lax.fori_loop(0, NODES // 64, latent_norm, 0)

    local[5].wait()
    local[6].wait()
    kvp[WIN : WIN + NODES, :] = jnp.dot(
        node[...], pw[...], preferred_element_type=F32
    ).astype(BF16)

    def kv_copy(k):
        source, target = ((NODES, 0), (WIN, WIN + NODES))[k]
        return pltpu.make_async_remote_copy(
            src_ref=kvp.at[pl.ds(source, WIN), :], dst_ref=kvp.at[pl.ds(target, WIN), :],
            send_sem=kv_send.at[k], recv_sem=kv_recv.at[k],
            device_id={"band": (up, down)[k], "mp": m}, device_id_type=MESH,
        )

    for k in range(2):
        kv_copy(k).start()
    local[7].wait()
    query = jnp.dot(node[...], pq[...], preferred_element_type=F32).astype(BF16) * BF16(0.125)
    local[4].wait()
    spread_p.collect()
    for k in range(2):
        kv_copy(k).wait_recv()

    span = NODES + 2 * WIN
    vals[0:span, 0:COLS] = kvp[:, COLS:]
    i = lax.broadcasted_iota(jnp.int32, (NODES, span), 0)
    j = lax.broadcasted_iota(jnp.int32, (NODES, span), 1)
    other = b * NODES - WIN + j
    valid = (jnp.abs(i + WIN - j) <= WIN) & (other >= 0) & (other < bands * NODES)
    result, _ = two_heads(query, kvp[:, 0:COLS], vals[0:span, :], jnp.where(valid, 0.0, NEG))
    heads2[:, at_cols(slot * COLS)] = result

    ring_g.start()
    ring_g.relay()

    def mixed_first(n, carry):
        at = pl.ds(pl.multiple_of(n * 256, 256), 256)
        latent[:, at] = latent[:, at] + half_product(heads2, pwo_all, c, at)
        return carry

    def mixed_second(n, carry):
        at = pl.ds(pl.multiple_of(n * 256, 256), 256)
        out[:, at] = (latent[:, at] + half_product(heads2, pwo_all, 1 - c, at)).astype(BF16)
        return carry

    lax.fori_loop(0, 4, mixed_first, 0)
    ring_g.from_partner()
    spread_p.from_partner()
    lax.fori_loop(0, 4, mixed_second, 0)

    for mat in range(2):
        for k in range(3):
            for s in range(2):
                weight_x(mat, k, s).wait_send()
                for t in range(2):
                    weight_y(mat, k, s, t, parity).wait_send()
    for one in (spread_o, spread_p, ring_h, ring_g):
        one.drain()
    rows_to_partner(grid_own).wait_send()
    for d in range(3):
        q_copy(d).wait_send()
        stat_copy(d).wait_send()
        for xs in range(4):
            part_copy(xs, d).wait_send()
    for k in range(2):
        qr_copy(k).wait_send()
        kv_copy(k).wait_send()

    @pl.when(is_rim)
    def _():
        for one in edge_copies:
            one.wait_send()
        for xx in range(4):
            rim_stat_copy(xx).wait_send()
            for xs in range(4):
                rim_copy(xs, xx).wait_send()


def solution(mesh):
    bands = mesh.shape["band"]
    ring = RING if bands % RING == 0 else 2
    layers = bands // ring

    def step(
        grid_latent, grid_gain, hidden_in, hid_gain, enc_wq, enc_wk, enc_wv, enc_wo,
        enc_edges, enc_counts, proc_gain, proc_wq, proc_wk, proc_wv, proc_wo,
    ):
        counts = enc_counts.reshape(1, NODES)
        edges = enc_edges.T
        hbm = pl.BlockSpec(memory_space=pl.ANY)
        vmem = pl.BlockSpec(memory_space=pltpu.VMEM)
        dma = pltpu.SemaphoreType.DMA
        spread_sems = lambda n: [dma((3,)), dma((4,)), dma((3, n)), dma((4, n)), dma((2,))]
        ring_sems = [dma((7,)), dma((2, 4))]
        return pl.pallas_call(
            functools.partial(kernel, bands, ring),
            out_shape=jax.ShapeDtypeStruct((NODES, D), BF16),
            in_specs=[hbm] * 10 + [vmem] * 7,
            out_specs=vmem,
            scratch_shapes=[
                pltpu.VMEM((ROWS, D), BF16),
                pltpu.VMEM((2 * ROWS, D), BF16),
                pltpu.VMEM((NODES, D), BF16),
                pltpu.VMEM((4, D, 2 * COLS), BF16),
                pltpu.VMEM((4, NODES, COLS), BF16),
                pltpu.VMEM((4, NODES, COLS), BF16),
                pltpu.VMEM((2 * ROWS, COLS), BF16),
                pltpu.VMEM((2 * ROWS, 2 * COLS), BF16),
                pltpu.VMEM((NODES, 2 * ROWS), F32),
                pltpu.VMEM((NODES, ROWS), F32),
                pltpu.VMEM((SLOTS, NODES), jnp.int32),
                pltpu.VMEM((1, NODES), jnp.int32),
                pltpu.VMEM((NODES, COLS), BF16),
                pltpu.VMEM((4, NODES, COLS), BF16),
                pltpu.VMEM((NODES, 128), F32),
                pltpu.VMEM((2, 8, 128), F32),
                pltpu.VMEM((4, NODES, COLS), BF16),
                pltpu.VMEM((NODES, 128), F32),
                pltpu.VMEM((2, 8, 128), F32),
                pltpu.VMEM((128, 128), F32),
                pltpu.VMEM((6, 4, OWN, COLS), BF16),
                pltpu.VMEM((6, 8, 128), F32),
                pltpu.VMEM((NODES, D), BF16),
                pltpu.VMEM((8, COLS, D), BF16),
                pltpu.VMEM((8, COLS, D), BF16),
                pltpu.VMEM((NODES, D), F32),
                pltpu.VMEM((D, 2 * COLS), BF16),
                pltpu.VMEM((D, COLS), BF16),
                pltpu.VMEM((NODES + 2 * WIN, 2 * COLS), BF16),
                pltpu.VMEM((NODES, D), BF16),
            ]
            + [dma((2, 3, 2)), dma((2, 4, 2)), dma((2, 3, 2, 2)), dma((2, 4, 2, 2))]
            + spread_sems(layers) * 2
            + ring_sems * 2
            + [
                dma((8,)),
                dma((2,)),
                dma((2, 2)),
                dma((3,)), dma((4,)),
                dma((2,)), dma((4,)),
                dma((3, 4)), dma((6, 4)),
                dma((3,)), dma((6,)),
                dma((4, 4)), dma((4,)),
                dma((2,)), dma((2,)),
            ],
            compiler_params=pltpu.CompilerParams(
                collective_id=0, has_side_effects=True, vmem_limit_bytes=60 * 1024 * 1024
            ),
        )(
            grid_latent, enc_wk, enc_wv, enc_wo, proc_wk, proc_wv, proc_wq, proc_wo, edges, counts,
            grid_gain.reshape(1, D), hidden_in, hid_gain.reshape(1, D), enc_wq, edges, counts,
            proc_gain.reshape(1, D),
        )

    return jax.shard_map(
        step,
        mesh=mesh,
        in_specs=(
            P(("band", "mp"), None), P(), P("band", None), P(),
            P(None, "mp"), P(None, "mp"), P(None, "mp"), P("mp", None),
            P("band", None), P("band"), P(),
            P(None, "mp"), P(None, "mp"), P(None, "mp"), P("mp", None),
        ),
        out_specs=P("band", None),
        check_vma=False,
    )
```

```python
import functools

import jax
import jax.numpy as jnp
from jax import lax
from jax.experimental import pallas as pl
from jax.experimental.pallas import tpu as pltpu
from jax.sharding import PartitionSpec as P

MESH = pl.DeviceIdType.MESH
EPSILON = 1e-05
NEG = -1e30
F32 = jnp.float32
BF16 = jnp.bfloat16

D = 1024
CHIPS = 4
ROWS = 512
NODES = 256
SLOTS = 32
WIN = 128
COLS = 128
HALF = 64
OWN = NODES // CHIPS
RING = 8


def norm_rows(values, gain):
    values = values.astype(F32)
    center = values - jnp.mean(values, axis=-1, keepdims=True)
    spread = jnp.mean(center * center, axis=-1, keepdims=True)
    return center * lax.rsqrt(spread + EPSILON) * gain


def at_cols(start):
    return pl.ds(pl.multiple_of(start, COLS), COLS)


class Ring:
    def __init__(self, place, send, recv, x, c):
        self.place, self.send, self.recv, self.x, self.c = place, send, recv, x, c
        self.others = [lax.rem(x + d, 4) for d in (3, 1, 2)]

    def copy(self, c, x, kind, device):
        ref = self.place(c, x)
        return pltpu.make_async_remote_copy(
            src_ref=ref, dst_ref=ref, send_sem=self.send.at[kind], recv_sem=self.recv.at[c, x],
            device_id={"mp": device}, device_id_type=MESH,
        )

    def sends(self):
        return [self.copy(self.c, self.x, k, 2 * xx + self.c) for k, xx in enumerate(self.others)]

    def to_partner(self, k):
        xx = self.x if k == 3 else self.others[k]
        return self.copy(self.c, xx, 3 + k, 2 * self.x + 1 - self.c)

    def start(self):
        for one in self.sends():
            one.start()
        self.to_partner(3).start()

    def relay(self):
        for k, xx in enumerate(self.others):
            self.copy(self.c, xx, k, 2 * xx + self.c).wait_recv()
            self.to_partner(k).start()

    def from_partner(self):
        for xx in range(4):
            self.copy(1 - self.c, xx, 0, 2 * self.x + 1 - self.c).wait_recv()

    def drain(self):
        for one in self.sends():
            one.wait_send()
        for k in range(4):
            self.to_partner(k).wait_send()


class Spread:
    def __init__(self, source, held, n, index, band_of, x, c, m, sems):
        self.source, self.held, self.n, self.index, self.band_of = source, held, n, index, band_of
        self.x, self.c, self.m = x, c, m
        self.x_send, self.x_recv, self.r_send, self.r_recv, self.p_sem = sems
        self.others = [lax.rem(x + d, 4) for d in (3, 1, 2)]
        self.rows = COLS // n

    def at(self, i):
        return pl.ds(pl.multiple_of(i * self.rows, self.rows), self.rows)

    def over_x(self, k):
        return pltpu.make_async_remote_copy(
            src_ref=self.source.at[self.at(self.index), :],
            dst_ref=self.held.at[self.c * 4 + self.x, self.at(self.index), :],
            send_sem=self.x_send.at[k], recv_sem=self.x_recv.at[self.x],
            device_id={"mp": 2 * self.others[k] + self.c}, device_id_type=MESH,
        )

    def piece(self, k, i, sem, recv, band):
        ref = self.held.at[self.c * 4 + self.others[k], self.at(i), :]
        return pltpu.make_async_remote_copy(
            src_ref=ref, dst_ref=ref, send_sem=sem, recv_sem=recv,
            device_id={"band": band, "mp": self.m}, device_id_type=MESH,
        )

    def along(self, k, d):
        i = lax.rem(self.index + d, self.n)
        return self.piece(
            k, self.index, self.r_send.at[k, d], self.r_recv.at[self.others[k], self.index], self.band_of(i)
        )

    def start(self):
        for k in range(3):
            self.over_x(k).start()

    def spread(self):
        for k in range(3):
            self.piece(
                k, self.index, self.r_send.at[k, 0], self.x_recv.at[self.others[k]], self.band_of(self.index)
            ).wait_recv()
        for d in range(1, self.n):
            for k in range(3):
                self.along(k, d).start()

    def to_partner(self, c):
        ref = self.held.at[pl.ds(c * 4, 4)]
        return pltpu.make_async_remote_copy(
            src_ref=ref, dst_ref=ref, send_sem=self.p_sem.at[0], recv_sem=self.p_sem.at[1],
            device_id={"mp": 2 * self.x + 1 - self.c}, device_id_type=MESH,
        )

    def collect(self):
        for k in range(3):
            for d in range(1, self.n):
                i = lax.rem(self.index + d, self.n)
                self.piece(
                    k, i, self.r_send.at[k, 0], self.r_recv.at[self.others[k], i], self.band_of(i)
                ).wait_recv()
        self.to_partner(self.c).start()

    def from_partner(self):
        self.to_partner(1 - self.c).wait_recv()

    def drain(self):
        for k in range(3):
            self.over_x(k).wait_send()
            for d in range(1, self.n):
                self.along(k, d).wait_send()
        self.to_partner(self.c).wait_send()


def code_of(index):
    high = jnp.clip(index >> 7, 0, 7)
    return ((COLS + (index & 127)) << high).astype(F32)


def sort_edges(edges_ref, counts_ref, columns_ref, base, width):
    slot = lax.broadcasted_iota(jnp.int32, (SLOTS, NODES), 0)
    index = edges_ref[...] - base
    live = (slot < counts_ref[...]) & (index >= 0) & (index < width)
    codes = jnp.where(live, code_of(index), -1.0)
    columns_ref[...] = jnp.concatenate([codes, jnp.full((COLS - SLOTS, NODES), -1.0, F32)], axis=0).T


def fill_bias(columns_ref, bias_ref, width):
    step = 16
    lane = lax.broadcasted_iota(jnp.int32, (step, COLS), 1)
    columns = [code_of(lane + k * COLS).astype(BF16) for k in range(width // COLS)]

    def block(i, carry):
        at = pl.ds(pl.multiple_of(i * step, step), step)
        edges = columns_ref[at, :]
        totals = [jnp.zeros((step, COLS), BF16) for _ in columns]
        for s in range(SLOTS):
            edge = jnp.broadcast_to(edges[:, s : s + 1], (step, COLS)).astype(BF16)
            totals = [
                total + jnp.where(edge == column, BF16(1), BF16(0)) for total, column in zip(totals, columns)
            ]
        for k, total in enumerate(totals):
            total = total.astype(F32)
            bias_ref[at, k * COLS : (k + 1) * COLS] = jnp.where(
                total > 0.0, jnp.log(jnp.maximum(total, 1.0)), NEG
            )
        return carry

    lax.fori_loop(0, NODES // step, block, 0)


def two_heads(query, keys, values, bias):
    first = lax.broadcasted_iota(jnp.int32, query.shape, 1) < HALF
    outs, sums = [], []
    for h in range(2):
        q = jnp.where(first if h == 0 else jnp.logical_not(first), query, jnp.zeros_like(query))
        scores = lax.dot_general(q, keys, (((1,), (1,)), ((), ())), preferred_element_type=F32) + bias
        top = jnp.max(scores, axis=1, keepdims=True)
        weights = jnp.exp(scores - top).astype(BF16)
        both = jnp.dot(weights, values, preferred_element_type=F32)
        total = both[:, COLS:]
        outs.append(both[:, :COLS] / total)
        sums.append(top + jnp.log(total))
    return jnp.where(first, outs[0], outs[1]).astype(BF16), sums


def kernel(
    bands, ring,
    grid, wk, wv, wo, pwk, pwv, pwq, pwo, edges_hbm, counts_hbm,
    grid_gain, hidden, hid_gain, wq, edges, counts, proc_gain,
    out,
    raw, normed, node, w, q, qr, keys, vals, bias, bias_r, edges_r, counts_r, columns,
    part, stat, stat_t, part_r, stat_r, stat_rt, spare, po, st, heads, wo_all, pwo_all, latent, pw, pq, kvp, heads2,
    wx_send, wx_recv, wy_send, wy_recv,
    o0, o1, o2, o3, o4, p0, p1, p2, p3, p4, hs, hr, gs, gr,
    loc, grid_sem, edge_sem, q_send, q_recv, qr_send, qr_recv,
    po_send, po_recv, st_send, st_recv, ro_send, rs_send, kv_send, kv_recv,
):
    b, m = lax.axis_index("band"), lax.axis_index("mp")
    x, c = lax.div(m, 2), lax.rem(m, 2)
    up, down = lax.rem(b + 1, bands), lax.rem(b + bands - 1, bands)
    is_top, is_low = x == 3, x == 0
    is_rim = jnp.logical_or(is_top, is_low)

    layers = bands // ring
    y, z = lax.rem(b, ring), lax.div(b, ring)
    parity = lax.rem(y, 2)

    def band_in_y(i):
        return z * ring + i

    def band_in_z(i):
        return i * ring + y

    ahead, behind = band_in_y(lax.rem(y + 1, ring)), band_in_y(lax.rem(y + ring - 1, ring))

    barrier = pltpu.get_barrier_semaphore()

    def greet(device):
        pl.semaphore_signal(barrier, inc=1, device_id=device, device_id_type=MESH)

    for d in range(1, 8):
        greet({"mp": lax.rem(m + d, 8)})
    for band in (up, down):
        for d in range(4):
            greet({"band": band, "mp": 2 * d + c})
    for d in range(1, ring):
        greet({"band": band_in_y(lax.rem(y + d, ring)), "mp": m})
    for d in range(1, layers):
        greet({"band": band_in_z(lax.rem(z + d, layers)), "mp": m})

    slot = c * 4 + x
    local = [
        pltpu.make_async_copy(wk, w.at[x, :, 0:COLS], loc.at[0]),
        pltpu.make_async_copy(wv, w.at[x, :, COLS:], loc.at[1]),
        pltpu.make_async_copy(grid, raw, loc.at[2]),
        pltpu.make_async_copy(wo, wo_all.at[slot], loc.at[3]),
        pltpu.make_async_copy(pwo, pwo_all.at[slot], loc.at[4]),
        pltpu.make_async_copy(pwk, pw.at[:, 0:COLS], loc.at[5]),
        pltpu.make_async_copy(pwv, pw.at[:, COLS:], loc.at[6]),
        pltpu.make_async_copy(pwq, pq, loc.at[7]),
    ]
    for one in local:
        one.start()
    pl.semaphore_wait(barrier, 13 + ring + layers)

    others = [lax.rem(x + d, 4) for d in (3, 1, 2)]

    def weight_part(xx, mat, row, count):
        return w.at[xx, pl.ds(pl.multiple_of(row, 128), count), pl.ds(mat * COLS, COLS)]

    def weight_x(mat, k, s):
        row = parity * 512 + s * 256
        return pltpu.make_async_remote_copy(
            src_ref=(wk, wv)[mat].at[pl.ds(pl.multiple_of(row, 256), 256), :],
            dst_ref=weight_part(x, mat, row, 256),
            send_sem=wx_send.at[mat, k, s], recv_sem=wx_recv.at[mat, x, s],
            device_id={"mp": 2 * others[k] + c}, device_id_type=MESH,
        )

    def weight_y(mat, k, s, t, half):
        ref = weight_part(others[k], mat, half * 512 + s * 256 + t * 128, 128)
        return pltpu.make_async_remote_copy(
            src_ref=ref, dst_ref=ref,
            send_sem=wy_send.at[mat, k, s, t], recv_sem=wy_recv.at[mat, others[k], s, t],
            device_id={"band": (ahead, behind)[t], "mp": m}, device_id_type=MESH,
        )

    def weight_relay(k, s):
        for mat in range(2):
            ref = weight_part(others[k], mat, parity * 512 + s * 256, 256)
            pltpu.make_async_remote_copy(
                src_ref=ref, dst_ref=ref,
                send_sem=wx_send.at[mat, k, s], recv_sem=wx_recv.at[mat, others[k], s],
                device_id={"mp": 2 * others[k] + c}, device_id_type=MESH,
            ).wait_recv()
            for t in range(2):
                weight_y(mat, k, s, t, parity).start()

    def weight_wait(k):
        for mat in range(2):
            for s in range(2):
                for t in range(2):
                    weight_y(mat, k, s, t, 1 - parity).wait_recv()

    spread_o = Spread(wo, wo_all, layers, z, band_in_z, x, c, m, (o0, o1, o2, o3, o4))
    spread_p = Spread(pwo, pwo_all, layers, z, band_in_z, x, c, m, (p0, p1, p2, p3, p4))

    def head_piece(cc, xx):
        return heads.at[
            pl.ds(pl.multiple_of(xx * OWN, OWN), OWN), pl.ds(pl.multiple_of(cc * 512, 512), 512)
        ]

    def out_piece(cc, xx):
        return heads2.at[:, at_cols((cc * 4 + xx) * COLS)]

    ring_h = Ring(head_piece, hs, hr, x, c)
    ring_g = Ring(out_piece, gs, gr, x, c)

    for mat in range(2):
        for k in range(2):
            weight_x(mat, k, 0).start()
    spread_o.start()
    for mat in range(2):
        for k in range(2):
            weight_x(mat, k, 1).start()
    grid_own = pl.ds(pl.multiple_of(c * ROWS, ROWS), ROWS)
    grid_other = pl.ds(pl.multiple_of((1 - c) * ROWS, ROWS), ROWS)

    def rows_to_partner(at):
        return pltpu.make_async_remote_copy(
            src_ref=normed.at[at, :], dst_ref=normed.at[at, :], send_sem=grid_sem.at[0], recv_sem=grid_sem.at[1],
            device_id={"mp": 2 * x + 1 - c}, device_id_type=MESH,
        )

    def rim_input(source, target, k, band):
        return pltpu.make_async_remote_copy(
            src_ref=source, dst_ref=target, send_sem=edge_sem.at[0, k], recv_sem=edge_sem.at[1, k],
            device_id={"band": band, "mp": m}, device_id_type=MESH,
        )

    rim_from = jnp.where(is_top, down, up)
    rim_to = jnp.where(is_top, up, down)
    edge_copies = [
        rim_input(edges_hbm, edges_r, 0, rim_from),
        rim_input(counts_hbm, counts_r, 1, rim_from),
    ]

    @pl.when(is_rim)
    def _():
        for one in edge_copies:
            one.start()

    def node_block(i, carry):
        at = pl.ds(pl.multiple_of(i * 64, 64), 64)
        node[at, :] = norm_rows(hidden[at, :], hid_gain[...]).astype(BF16)
        return carry

    lax.fori_loop(0, NODES // 64, node_block, 0)
    q[x] = jnp.dot(node[...], wq[...], preferred_element_type=F32).astype(BF16) * BF16(0.125)

    def q_copy(d):
        return pltpu.make_async_remote_copy(
            src_ref=q.at[x], dst_ref=q.at[x], send_sem=q_send.at[d], recv_sem=q_recv.at[x],
            device_id={"mp": 2 * lax.rem(x + d + 1, 4) + c}, device_id_type=MESH,
        )

    def qr_copy(k):
        return pltpu.make_async_remote_copy(
            src_ref=q.at[x], dst_ref=qr.at[x], send_sem=qr_send.at[k], recv_sem=qr_recv.at[x],
            device_id={"band": (down, up)[k], "mp": (6, 0)[k] + c}, device_id_type=MESH,
        )

    def q_arrival(ref, sems, xx):
        return pltpu.make_async_remote_copy(
            src_ref=ref.at[xx], dst_ref=ref.at[xx], send_sem=q_send.at[0], recv_sem=sems.at[xx],
            device_id={"mp": 2 * xx + c}, device_id_type=MESH,
        )

    for d in range(3):
        q_copy(d).start()
    for k in range(2):
        qr_copy(k).start()
    for mat in range(2):
        for s in range(2):
            weight_x(mat, 2, s).start()
    spread_p.start()

    def grid_block(i, carry):
        at = pl.ds(pl.multiple_of(i * 64, 64), 64)
        normed[pl.ds(pl.multiple_of(c * ROWS + i * 64, 64), 64), :] = norm_rows(raw[at, :], grid_gain[...]).astype(BF16)
        return carry

    base = b * (8 * ROWS) + x * (2 * ROWS)
    rim_row = jnp.where(is_top, ROWS, 0)
    local[2].wait()
    lax.fori_loop(0, ROWS // 64, grid_block, 0)
    rows_to_partner(grid_own).start()
    sort_edges(edges, counts, columns, base, 2 * ROWS)
    fill_bias(columns, bias, 2 * ROWS)
    weight_relay(0, 0)
    weight_relay(1, 0)
    spread_o.spread()
    vals[:, COLS:] = jnp.ones((2 * ROWS, COLS), BF16)
    stat[...] = jnp.zeros_like(stat)
    stat_r[...] = jnp.zeros_like(stat_r)

    @pl.when(is_rim)
    def _():
        for one in edge_copies:
            one.wait_recv()
        sort_edges(edges_r, counts_r, columns, base + rim_row, ROWS)
        fill_bias(columns, bias_r, ROWS)

    rows_to_partner(grid_other).wait_recv()

    def part_copy(xs, d):
        xx = lax.rem(x + d + 1, 4)
        return pltpu.make_async_remote_copy(
            src_ref=part.at[xs, pl.ds(pl.multiple_of(xx * OWN, OWN), OWN), :],
            dst_ref=po.at[x, xs],
            send_sem=po_send.at[d, xs], recv_sem=po_recv.at[x, xs],
            device_id={"mp": 2 * xx + c}, device_id_type=MESH,
        )

    rim_slot = jnp.where(is_top, 4, 5)

    def rim_copy(xs, xx):
        return pltpu.make_async_remote_copy(
            src_ref=part_r.at[xs, pl.ds(xx * OWN, OWN), :],
            dst_ref=po.at[rim_slot, xs],
            send_sem=ro_send.at[xx, xs], recv_sem=po_recv.at[rim_slot, xs],
            device_id={"band": rim_to, "mp": 2 * xx + c}, device_id_type=MESH,
        )

    def stat_copy(d):
        xx = lax.rem(x + d + 1, 4)
        return pltpu.make_async_remote_copy(
            src_ref=stat_t.at[lax.div(xx, 2)], dst_ref=st.at[x],
            send_sem=st_send.at[d], recv_sem=st_recv.at[x],
            device_id={"mp": 2 * xx + c}, device_id_type=MESH,
        )

    def rim_stat_copy(xx):
        return pltpu.make_async_remote_copy(
            src_ref=stat_rt.at[xx // 2], dst_ref=st.at[rim_slot],
            send_sem=rs_send.at[xx], recv_sem=st_recv.at[rim_slot],
            device_id={"band": rim_to, "mp": 2 * xx + c}, device_id_type=MESH,
        )

    chunk = 128

    def attend(xs, q_ref, bias_ref, part_ref, stat_ref, first_row, width):
        def block(i, carry):
            at = pl.ds(pl.multiple_of(i * chunk, chunk), chunk)
            span = pl.ds(pl.multiple_of(first_row, ROWS), width)
            result, sums = two_heads(q_ref[xs, at, :], keys[span, :], vals[span, :], bias_ref[at, :])
            part_ref[xs, at, :] = result
            lane = lax.broadcasted_iota(jnp.int32, (chunk, 128), 1)
            old = stat_ref[at, :]
            old = jnp.where(lane == 2 * xs, sums[0], old)
            stat_ref[at, :] = jnp.where(lane == 2 * xs + 1, sums[1], old)
            return carry

        lax.fori_loop(0, NODES // chunk, block, 0, unroll=True)

    def slice_of(xs):
        def project(i, inner):
            at = pl.ds(pl.multiple_of(i * ROWS, ROWS), ROWS)
            both = jnp.dot(normed[at, :], w[xs], preferred_element_type=F32).astype(BF16)
            keys[at, :] = both[:, :COLS]
            vals[at, 0:COLS] = both[:, COLS:]
            return inner

        lax.fori_loop(0, 2, project, 0)

        @pl.when(is_rim)
        def _():
            q_arrival(qr, qr_recv, xs).wait_recv()
            attend(xs, qr, bias_r, part_r, stat_r, rim_row, ROWS)
            for xx in range(4):
                rim_copy(xs, xx).start()

        attend(xs, q, bias, part, stat, 0, 2 * ROWS)
        for d in range(3):
            part_copy(xs, d).start()

    def head_step(j, carry):
        xs = lax.rem(x + jnp.where(j == 1, 3, jnp.where(j == 2, 1, 2)), 4)
        for k in range(3):

            @pl.when(j == k + 1)
            def _():
                weight_wait(k)

        @pl.when(j == 2)
        def _():
            weight_relay(2, 0)
            weight_relay(2, 1)

        q_arrival(q, q_recv, xs).wait_recv()
        slice_of(xs)
        return carry

    local[0].wait()
    local[1].wait()
    slice_of(x)
    weight_relay(0, 1)
    weight_relay(1, 1)
    lax.fori_loop(1, 4, head_step, 0)

    for half in range(2):
        stat_t[half] = stat[half * 128 : half * 128 + 128, :].T[0:8]
    for d in range(3):
        stat_copy(d).start()

    @pl.when(is_rim)
    def _():
        for half in range(2):
            stat_rt[half] = stat_r[half * 128 : half * 128 + 128, :].T[0:8]
        for xx in range(4):
            rim_stat_copy(xx).start()

    spread_p.spread()
    mine = pl.ds(pl.multiple_of(x * OWN, OWN), OWN)
    st[x] = stat_t[lax.div(x, 2)]
    for xs in range(4):
        po[x, xs] = part[xs, mine, :]

    def arrivals(i):
        for xs in range(4):
            pltpu.make_async_remote_copy(
                src_ref=po.at[i, xs], dst_ref=po.at[i, xs],
                send_sem=po_send.at[0, xs], recv_sem=po_recv.at[i, xs],
                device_id={"mp": m}, device_id_type=MESH,
            ).wait_recv()
        pltpu.make_async_remote_copy(
            src_ref=st.at[i], dst_ref=st.at[i], send_sem=st_send.at[0], recv_sem=st_recv.at[i],
            device_id={"mp": m}, device_id_type=MESH,
        ).wait_recv()

    for d in range(3):
        arrivals(lax.rem(x + d + 1, 4))
    arrivals(4)
    arrivals(5)

    top = st[0]
    for i in range(1, 6):
        top = jnp.maximum(top, st[i])
    shares = [jnp.exp(st[i] - top) for i in range(6)]
    whole = shares[0]
    for i in range(1, 6):
        whole = whole + shares[i]
    shares = [one / whole for one in shares]
    spare[...] = jnp.concatenate(shares + [jnp.zeros((128 - 48, 128), F32)], axis=0).T
    share = spare[pl.ds(pl.multiple_of(lax.rem(x, 2) * OWN, OWN), OWN), :]
    first = lax.broadcasted_iota(jnp.int32, (OWN, COLS), 1) < HALF
    for xs in range(4):
        total = jnp.zeros((OWN, COLS), F32)
        for i in range(6):
            at = i * 8 + 2 * xs
            left = jnp.broadcast_to(share[:, at : at + 1], (OWN, COLS))
            right = jnp.broadcast_to(share[:, at + 1 : at + 2], (OWN, COLS))
            total = total + jnp.where(first, left, right) * po[i, xs].astype(F32)
        heads[mine, at_cols(c * 512 + xs * COLS)] = total.astype(BF16)

    ring_h.start()
    ring_h.relay()
    local[3].wait()
    spread_o.collect()

    def half_product(left, right, cc, at):
        return jnp.dot(
            left[:, pl.ds(pl.multiple_of(cc * 512, 512), 512)],
            right[pl.ds(cc * 4, 4), :, at].reshape(512, 256),
            preferred_element_type=F32,
        )

    def latent_first(n, carry):
        at = pl.ds(pl.multiple_of(n * 256, 256), 256)
        latent[:, at] = hidden[:, at].astype(F32) + half_product(heads, wo_all, c, at)
        return carry

    def latent_second(n, carry):
        at = pl.ds(pl.multiple_of(n * 256, 256), 256)
        latent[:, at] = latent[:, at] + half_product(heads, wo_all, 1 - c, at)
        return carry

    lax.fori_loop(0, 4, latent_first, 0, unroll=True)
    ring_h.from_partner()
    spread_o.from_partner()
    lax.fori_loop(0, 4, latent_second, 0, unroll=True)

    def latent_norm(i, carry):
        at = pl.ds(pl.multiple_of(i * 64, 64), 64)
        node[at, :] = norm_rows(latent[at, :], proc_gain[...]).astype(BF16)
        return carry

    lax.fori_loop(0, NODES // 64, latent_norm, 0)

    local[5].wait()
    local[6].wait()
    kvp[WIN : WIN + NODES, :] = jnp.dot(
        node[...], pw[...], preferred_element_type=F32
    ).astype(BF16)

    def kv_copy(k):
        source, target = ((NODES, 0), (WIN, WIN + NODES))[k]
        return pltpu.make_async_remote_copy(
            src_ref=kvp.at[pl.ds(source, WIN), :], dst_ref=kvp.at[pl.ds(target, WIN), :],
            send_sem=kv_send.at[k], recv_sem=kv_recv.at[k],
            device_id={"band": (up, down)[k], "mp": m}, device_id_type=MESH,
        )

    for k in range(2):
        kv_copy(k).start()
    local[7].wait()
    query = jnp.dot(node[...], pq[...], preferred_element_type=F32).astype(BF16) * BF16(0.125)
    local[4].wait()
    spread_p.collect()
    for k in range(2):
        kv_copy(k).wait_recv()

    span = NODES + 2 * WIN
    vals[0:span, 0:COLS] = kvp[:, COLS:]
    i = lax.broadcasted_iota(jnp.int32, (NODES, span), 0)
    j = lax.broadcasted_iota(jnp.int32, (NODES, span), 1)
    other = b * NODES - WIN + j
    valid = (jnp.abs(i + WIN - j) <= WIN) & (other >= 0) & (other < bands * NODES)
    result, _ = two_heads(query, kvp[:, 0:COLS], vals[0:span, :], jnp.where(valid, 0.0, NEG))
    heads2[:, at_cols(slot * COLS)] = result

    ring_g.start()
    for mat in range(2):
        for k in range(3):
            for s in range(2):
                weight_x(mat, k, s).wait_send()
                for t in range(2):
                    weight_y(mat, k, s, t, parity).wait_send()
    for one in (spread_o, spread_p, ring_h):
        one.drain()
    rows_to_partner(grid_own).wait_send()
    for d in range(3):
        q_copy(d).wait_send()
        stat_copy(d).wait_send()
        for xs in range(4):
            part_copy(xs, d).wait_send()
    for k in range(2):
        qr_copy(k).wait_send()
        kv_copy(k).wait_send()

    @pl.when(is_rim)
    def _():
        for one in edge_copies:
            one.wait_send()
        for xx in range(4):
            rim_stat_copy(xx).wait_send()
            for xs in range(4):
                rim_copy(xs, xx).wait_send()

    ring_g.relay()

    def mixed_first(n, carry):
        at = pl.ds(pl.multiple_of(n * 256, 256), 256)
        latent[:, at] = latent[:, at] + half_product(heads2, pwo_all, c, at)
        return carry

    def mixed_second(n, carry):
        at = pl.ds(pl.multiple_of(n * 256, 256), 256)
        out[:, at] = (latent[:, at] + half_product(heads2, pwo_all, 1 - c, at)).astype(BF16)
        return carry

    lax.fori_loop(0, 4, mixed_first, 0, unroll=True)
    ring_g.from_partner()
    spread_p.from_partner()
    lax.fori_loop(0, 4, mixed_second, 0, unroll=True)

    ring_g.drain()


def solution(mesh):
    bands = mesh.shape["band"]
    ring = RING if bands % RING == 0 else 2
    layers = bands // ring

    def step(
        grid_latent, grid_gain, hidden_in, hid_gain, enc_wq, enc_wk, enc_wv, enc_wo,
        enc_edges, enc_counts, proc_gain, proc_wq, proc_wk, proc_wv, proc_wo,
    ):
        counts = enc_counts.reshape(1, NODES)
        edges = enc_edges.T
        hbm = pl.BlockSpec(memory_space=pl.ANY)
        vmem = pl.BlockSpec(memory_space=pltpu.VMEM)
        dma = pltpu.SemaphoreType.DMA
        spread_sems = lambda n: [dma((3,)), dma((4,)), dma((3, n)), dma((4, n)), dma((2,))]
        ring_sems = [dma((7,)), dma((2, 4))]
        return pl.pallas_call(
            functools.partial(kernel, bands, ring),
            out_shape=jax.ShapeDtypeStruct((NODES, D), BF16),
            in_specs=[hbm] * 10 + [vmem] * 7,
            out_specs=vmem,
            scratch_shapes=[
                pltpu.VMEM((ROWS, D), BF16),
                pltpu.VMEM((2 * ROWS, D), BF16),
                pltpu.VMEM((NODES, D), BF16),
                pltpu.VMEM((4, D, 2 * COLS), BF16),
                pltpu.VMEM((4, NODES, COLS), BF16),
                pltpu.VMEM((4, NODES, COLS), BF16),
                pltpu.VMEM((2 * ROWS, COLS), BF16),
                pltpu.VMEM((2 * ROWS, 2 * COLS), BF16),
                pltpu.VMEM((NODES, 2 * ROWS), F32),
                pltpu.VMEM((NODES, ROWS), F32),
                pltpu.VMEM((SLOTS, NODES), jnp.int32),
                pltpu.VMEM((1, NODES), jnp.int32),
                pltpu.VMEM((NODES, COLS), F32),
                pltpu.VMEM((4, NODES, COLS), BF16),
                pltpu.VMEM((NODES, 128), F32),
                pltpu.VMEM((2, 8, 128), F32),
                pltpu.VMEM((4, NODES, COLS), BF16),
                pltpu.VMEM((NODES, 128), F32),
                pltpu.VMEM((2, 8, 128), F32),
                pltpu.VMEM((128, 128), F32),
                pltpu.VMEM((6, 4, OWN, COLS), BF16),
                pltpu.VMEM((6, 8, 128), F32),
                pltpu.VMEM((NODES, D), BF16),
                pltpu.VMEM((8, COLS, D), BF16),
                pltpu.VMEM((8, COLS, D), BF16),
                pltpu.VMEM((NODES, D), F32),
                pltpu.VMEM((D, 2 * COLS), BF16),
                pltpu.VMEM((D, COLS), BF16),
                pltpu.VMEM((NODES + 2 * WIN, 2 * COLS), BF16),
                pltpu.VMEM((NODES, D), BF16),
            ]
            + [dma((2, 3, 2)), dma((2, 4, 2)), dma((2, 3, 2, 2)), dma((2, 4, 2, 2))]
            + spread_sems(layers) * 2
            + ring_sems * 2
            + [
                dma((8,)),
                dma((2,)),
                dma((2, 2)),
                dma((3,)), dma((4,)),
                dma((2,)), dma((4,)),
                dma((3, 4)), dma((6, 4)),
                dma((3,)), dma((6,)),
                dma((4, 4)), dma((4,)),
                dma((2,)), dma((2,)),
            ],
            compiler_params=pltpu.CompilerParams(
                collective_id=0, has_side_effects=True, vmem_limit_bytes=60 * 1024 * 1024
            ),
        )(
            grid_latent, enc_wk, enc_wv, enc_wo, proc_wk, proc_wv, proc_wq, proc_wo, edges, counts,
            grid_gain.reshape(1, D), hidden_in, hid_gain.reshape(1, D), enc_wq, edges, counts,
            proc_gain.reshape(1, D),
        )

    return jax.shard_map(
        step,
        mesh=mesh,
        in_specs=(
            P(("band", "mp"), None), P(), P("band", None), P(),
            P(None, "mp"), P(None, "mp"), P(None, "mp"), P("mp", None),
            P("band", None), P("band"), P(),
            P(None, "mp"), P(None, "mp"), P(None, "mp"), P("mp", None),
        ),
        out_specs=P("band", None),
        check_vma=False,
    )
```

```python
import functools

import jax
import jax.numpy as jnp
from jax import lax
from jax.experimental import pallas as pl
from jax.experimental.pallas import tpu as pltpu
from jax.sharding import PartitionSpec as P

MESH = pl.DeviceIdType.MESH
EPSILON = 1e-05
NEG = -1e30
F32 = jnp.float32
BF16 = jnp.bfloat16

D = 1024
CHIPS = 4
ROWS = 512
NODES = 256
SLOTS = 32
WIN = 128
COLS = 128
HALF = 64
OWN = NODES // CHIPS
RING = 8


def norm_rows(values, gain):
    values = values.astype(F32)
    center = values - jnp.mean(values, axis=-1, keepdims=True)
    spread = jnp.mean(center * center, axis=-1, keepdims=True)
    return center * lax.rsqrt(spread + EPSILON) * gain


def at_cols(start):
    return pl.ds(pl.multiple_of(start, COLS), COLS)


class Ring:
    def __init__(self, place, send, recv, x, c):
        self.place, self.send, self.recv, self.x, self.c = place, send, recv, x, c
        self.others = [lax.rem(x + d, 4) for d in (3, 1, 2)]

    def copy(self, c, x, kind, device):
        ref = self.place(c, x)
        return pltpu.make_async_remote_copy(
            src_ref=ref, dst_ref=ref, send_sem=self.send.at[kind], recv_sem=self.recv.at[c, x],
            device_id={"mp": device}, device_id_type=MESH,
        )

    def sends(self):
        return [self.copy(self.c, self.x, k, 2 * xx + self.c) for k, xx in enumerate(self.others)]

    def to_partner(self, k):
        xx = self.x if k == 3 else self.others[k]
        return self.copy(self.c, xx, 3 + k, 2 * self.x + 1 - self.c)

    def start(self):
        for one in self.sends():
            one.start()
        self.to_partner(3).start()

    def relay(self):
        for k, xx in enumerate(self.others):
            self.copy(self.c, xx, k, 2 * xx + self.c).wait_recv()
            self.to_partner(k).start()

    def from_partner(self):
        for xx in range(4):
            self.copy(1 - self.c, xx, 0, 2 * self.x + 1 - self.c).wait_recv()

    def drain(self):
        for one in self.sends():
            one.wait_send()
        for k in range(4):
            self.to_partner(k).wait_send()


class Spread:
    def __init__(self, source, held, n, index, band_of, x, c, m, sems):
        self.source, self.held, self.n, self.index, self.band_of = source, held, n, index, band_of
        self.x, self.c, self.m = x, c, m
        self.x_send, self.x_recv, self.r_send, self.r_recv, self.p_sem = sems
        self.others = [lax.rem(x + d, 4) for d in (3, 1, 2)]
        self.rows = COLS // n

    def at(self, i):
        return pl.ds(pl.multiple_of(i * self.rows, self.rows), self.rows)

    def over_x(self, k):
        return pltpu.make_async_remote_copy(
            src_ref=self.source.at[self.at(self.index), :],
            dst_ref=self.held.at[self.c * 4 + self.x, self.at(self.index), :],
            send_sem=self.x_send.at[k], recv_sem=self.x_recv.at[self.x],
            device_id={"mp": 2 * self.others[k] + self.c}, device_id_type=MESH,
        )

    def piece(self, k, i, sem, recv, band):
        ref = self.held.at[self.c * 4 + self.others[k], self.at(i), :]
        return pltpu.make_async_remote_copy(
            src_ref=ref, dst_ref=ref, send_sem=sem, recv_sem=recv,
            device_id={"band": band, "mp": self.m}, device_id_type=MESH,
        )

    def along(self, k, d):
        i = lax.rem(self.index + d, self.n)
        return self.piece(
            k, self.index, self.r_send.at[k, d], self.r_recv.at[self.others[k], self.index], self.band_of(i)
        )

    def start(self):
        for k in range(3):
            self.over_x(k).start()

    def spread(self):
        for k in range(3):
            self.piece(
                k, self.index, self.r_send.at[k, 0], self.x_recv.at[self.others[k]], self.band_of(self.index)
            ).wait_recv()
        for d in range(1, self.n):
            for k in range(3):
                self.along(k, d).start()

    def to_partner(self, c):
        ref = self.held.at[pl.ds(c * 4, 4)]
        return pltpu.make_async_remote_copy(
            src_ref=ref, dst_ref=ref, send_sem=self.p_sem.at[0], recv_sem=self.p_sem.at[1],
            device_id={"mp": 2 * self.x + 1 - self.c}, device_id_type=MESH,
        )

    def collect(self):
        for k in range(3):
            for d in range(1, self.n):
                i = lax.rem(self.index + d, self.n)
                self.piece(
                    k, i, self.r_send.at[k, 0], self.r_recv.at[self.others[k], i], self.band_of(i)
                ).wait_recv()
        self.to_partner(self.c).start()

    def from_partner(self):
        self.to_partner(1 - self.c).wait_recv()

    def drain(self):
        for k in range(3):
            self.over_x(k).wait_send()
            for d in range(1, self.n):
                self.along(k, d).wait_send()
        self.to_partner(self.c).wait_send()


def code_of(index):
    high = jnp.clip(index >> 7, 0, 7)
    return ((COLS + (index & 127)) << high).astype(F32)


def sort_edges(edges_ref, counts_ref, columns_ref, base, width):
    slot = lax.broadcasted_iota(jnp.int32, (SLOTS, NODES), 0)
    index = edges_ref[...] - base
    live = (slot < counts_ref[...]) & (index >= 0) & (index < width)
    codes = jnp.where(live, code_of(index), -1.0)
    columns_ref[...] = jnp.concatenate([codes, jnp.full((COLS - SLOTS, NODES), -1.0, F32)], axis=0).T


def fill_bias(columns_ref, bias_ref, width):
    step = 16
    lane = lax.broadcasted_iota(jnp.int32, (step, COLS), 1)
    columns = [code_of(lane + k * COLS).astype(BF16) for k in range(width // COLS)]

    def block(i, carry):
        at = pl.ds(pl.multiple_of(i * step, step), step)
        edges = columns_ref[at, :]
        totals = [jnp.zeros((step, COLS), BF16) for _ in columns]
        for s in range(SLOTS):
            edge = jnp.broadcast_to(edges[:, s : s + 1], (step, COLS)).astype(BF16)
            totals = [
                total + jnp.where(edge == column, BF16(1), BF16(0)) for total, column in zip(totals, columns)
            ]
        for k, total in enumerate(totals):
            total = total.astype(F32)
            bias_ref[at, k * COLS : (k + 1) * COLS] = jnp.where(
                total > 0.0, jnp.log(jnp.maximum(total, 1.0)), NEG
            )
        return carry

    lax.fori_loop(0, NODES // step, block, 0)


def two_heads(query, keys, values, bias):
    first = lax.broadcasted_iota(jnp.int32, query.shape, 1) < HALF
    outs, sums = [], []
    for h in range(2):
        q = jnp.where(first if h == 0 else jnp.logical_not(first), query, jnp.zeros_like(query))
        scores = lax.dot_general(q, keys, (((1,), (1,)), ((), ())), preferred_element_type=F32) + bias
        top = jnp.max(scores, axis=1, keepdims=True)
        weights = jnp.exp(scores - top).astype(BF16)
        both = jnp.dot(weights, values, preferred_element_type=F32)
        total = both[:, COLS:]
        outs.append(both[:, :COLS] / total)
        sums.append(top + jnp.log(total))
    return jnp.where(first, outs[0], outs[1]).astype(BF16), sums


def kernel(
    bands, ring,
    grid, wk, wv, wo, pwk, pwv, pwq, pwo, edges_hbm, counts_hbm,
    grid_gain, hidden, hid_gain, wq, edges, counts, proc_gain,
    out,
    raw, normed, node, w, q, qr, keys, vals, bias, bias_r, edges_r, counts_r, columns,
    part, stat, stat_t, part_r, stat_r, stat_rt, spare, po, st, heads, wo_all, pwo_all, latent, pw, pq, kvp, heads2,
    wx_send, wx_recv, wy_send, wy_recv,
    o0, o1, o2, o3, o4, p0, p1, p2, p3, p4, hs, hr, gs, gr,
    loc, grid_sem, edge_sem, q_send, q_recv, qr_send, qr_recv, out_sem,
    po_send, po_recv, st_send, st_recv, ro_send, rs_send, kv_send, kv_recv,
):
    b, m = lax.axis_index("band"), lax.axis_index("mp")
    x, c = lax.div(m, 2), lax.rem(m, 2)
    up, down = lax.rem(b + 1, bands), lax.rem(b + bands - 1, bands)
    is_top, is_low = x == 3, x == 0
    is_rim = jnp.logical_or(is_top, is_low)

    layers = bands // ring
    y, z = lax.rem(b, ring), lax.div(b, ring)
    parity = lax.rem(y, 2)

    def band_in_y(i):
        return z * ring + i

    def band_in_z(i):
        return i * ring + y

    ahead, behind = band_in_y(lax.rem(y + 1, ring)), band_in_y(lax.rem(y + ring - 1, ring))

    barrier = pltpu.get_barrier_semaphore()

    def greet(device):
        pl.semaphore_signal(barrier, inc=1, device_id=device, device_id_type=MESH)

    for d in range(1, 8):
        greet({"mp": lax.rem(m + d, 8)})
    for band in (up, down):
        for d in range(4):
            greet({"band": band, "mp": 2 * d + c})
    for d in range(1, ring):
        greet({"band": band_in_y(lax.rem(y + d, ring)), "mp": m})
    for d in range(1, layers):
        greet({"band": band_in_z(lax.rem(z + d, layers)), "mp": m})

    slot = c * 4 + x
    local = [
        pltpu.make_async_copy(wk, w.at[x, :, 0:COLS], loc.at[0]),
        pltpu.make_async_copy(wv, w.at[x, :, COLS:], loc.at[1]),
        pltpu.make_async_copy(grid, raw, loc.at[2]),
        pltpu.make_async_copy(wo, wo_all.at[slot], loc.at[3]),
        pltpu.make_async_copy(pwo, pwo_all.at[slot], loc.at[4]),
        pltpu.make_async_copy(pwk, pw.at[:, 0:COLS], loc.at[5]),
        pltpu.make_async_copy(pwv, pw.at[:, COLS:], loc.at[6]),
        pltpu.make_async_copy(pwq, pq, loc.at[7]),
    ]
    for one in local:
        one.start()
    def node_block(i, carry):
        at = pl.ds(pl.multiple_of(i * 64, 64), 64)
        node[at, :] = norm_rows(hidden[at, :], hid_gain[...]).astype(BF16)
        return carry

    lax.fori_loop(0, NODES // 64, node_block, 0)
    q[x] = jnp.dot(node[...], wq[...], preferred_element_type=F32).astype(BF16) * BF16(0.125)

    def grid_block(i, carry):
        at = pl.ds(pl.multiple_of(i * 64, 64), 64)
        normed[pl.ds(pl.multiple_of(c * ROWS + i * 64, 64), 64), :] = norm_rows(raw[at, :], grid_gain[...]).astype(BF16)
        return carry

    local[2].wait()
    lax.fori_loop(0, ROWS // 64, grid_block, 0)
    pl.semaphore_wait(barrier, 13 + ring + layers)


    others = [lax.rem(x + d, 4) for d in (3, 1, 2)]

    def weight_part(xx, mat, row, count):
        return w.at[xx, pl.ds(pl.multiple_of(row, 128), count), pl.ds(mat * COLS, COLS)]

    def weight_x(mat, k, s):
        row = parity * 512 + s * 256
        return pltpu.make_async_remote_copy(
            src_ref=(wk, wv)[mat].at[pl.ds(pl.multiple_of(row, 256), 256), :],
            dst_ref=weight_part(x, mat, row, 256),
            send_sem=wx_send.at[mat, k, s], recv_sem=wx_recv.at[mat, x, s],
            device_id={"mp": 2 * others[k] + c}, device_id_type=MESH,
        )

    def weight_y(mat, k, s, t, half):
        ref = weight_part(others[k], mat, half * 512 + s * 256 + t * 128, 128)
        return pltpu.make_async_remote_copy(
            src_ref=ref, dst_ref=ref,
            send_sem=wy_send.at[mat, k, s, t], recv_sem=wy_recv.at[mat, others[k], s, t],
            device_id={"band": (ahead, behind)[t], "mp": m}, device_id_type=MESH,
        )

    def weight_relay(k, s):
        for mat in range(2):
            ref = weight_part(others[k], mat, parity * 512 + s * 256, 256)
            pltpu.make_async_remote_copy(
                src_ref=ref, dst_ref=ref,
                send_sem=wx_send.at[mat, k, s], recv_sem=wx_recv.at[mat, others[k], s],
                device_id={"mp": 2 * others[k] + c}, device_id_type=MESH,
            ).wait_recv()
            for t in range(2):
                weight_y(mat, k, s, t, parity).start()

    def weight_wait(k):
        for mat in range(2):
            for s in range(2):
                for t in range(2):
                    weight_y(mat, k, s, t, 1 - parity).wait_recv()

    spread_o = Spread(wo, wo_all, layers, z, band_in_z, x, c, m, (o0, o1, o2, o3, o4))
    spread_p = Spread(pwo, pwo_all, layers, z, band_in_z, x, c, m, (p0, p1, p2, p3, p4))

    def head_piece(cc, xx):
        return heads.at[
            pl.ds(pl.multiple_of(xx * OWN, OWN), OWN), pl.ds(pl.multiple_of(cc * 512, 512), 512)
        ]

    def out_piece(cc, xx):
        return heads2.at[:, at_cols((cc * 4 + xx) * COLS)]

    ring_h = Ring(head_piece, hs, hr, x, c)
    ring_g = Ring(out_piece, gs, gr, x, c)

    grid_own = pl.ds(pl.multiple_of(c * ROWS, ROWS), ROWS)
    grid_other = pl.ds(pl.multiple_of((1 - c) * ROWS, ROWS), ROWS)

    def rows_to_partner(at):
        return pltpu.make_async_remote_copy(
            src_ref=normed.at[at, :], dst_ref=normed.at[at, :], send_sem=grid_sem.at[0], recv_sem=grid_sem.at[1],
            device_id={"mp": 2 * x + 1 - c}, device_id_type=MESH,
        )

    def rim_input(source, target, k, band):
        return pltpu.make_async_remote_copy(
            src_ref=source, dst_ref=target, send_sem=edge_sem.at[0, k], recv_sem=edge_sem.at[1, k],
            device_id={"band": band, "mp": m}, device_id_type=MESH,
        )

    rim_from = jnp.where(is_top, down, up)
    rim_to = jnp.where(is_top, up, down)
    edge_copies = [
        rim_input(edges_hbm, edges_r, 0, rim_from),
        rim_input(counts_hbm, counts_r, 1, rim_from),
    ]

    @pl.when(is_rim)
    def _():
        for one in edge_copies:
            one.start()

    def q_copy(d):
        return pltpu.make_async_remote_copy(
            src_ref=q.at[x], dst_ref=q.at[x], send_sem=q_send.at[d], recv_sem=q_recv.at[x],
            device_id={"mp": 2 * lax.rem(x + d + 1, 4) + c}, device_id_type=MESH,
        )

    outer = jnp.where(is_top, down, up)

    def qr_copy(xx):
        return pltpu.make_async_remote_copy(
            src_ref=q.at[xx], dst_ref=qr.at[xx], send_sem=qr_send.at[xx], recv_sem=qr_recv.at[xx],
            device_id={"band": outer, "mp": m}, device_id_type=MESH,
        )

    def q_arrival(ref, sems, xx):
        return pltpu.make_async_remote_copy(
            src_ref=ref.at[xx], dst_ref=ref.at[xx], send_sem=q_send.at[0], recv_sem=sems.at[xx],
            device_id={"mp": 2 * xx + c}, device_id_type=MESH,
        )

    for mat in range(2):
        for k in range(2):
            weight_x(mat, k, 0).start()
    rows_to_partner(grid_own).start()
    for d in range(3):
        q_copy(d).start()

    @pl.when(is_rim)
    def _():
        qr_copy(x).start()

    spread_o.start()
    for mat in range(2):
        for k in range(2):
            weight_x(mat, k, 1).start()
    for mat in range(2):
        for s in range(2):
            weight_x(mat, 2, s).start()
    spread_p.start()

    base = b * (8 * ROWS) + x * (2 * ROWS)
    rim_row = jnp.where(is_top, ROWS, 0)
    sort_edges(edges, counts, columns, base, 2 * ROWS)
    fill_bias(columns, bias, 2 * ROWS)
    weight_relay(0, 0)
    weight_relay(1, 0)
    vals[:, COLS:] = jnp.ones((2 * ROWS, COLS), BF16)
    stat[...] = jnp.zeros_like(stat)
    stat_r[...] = jnp.zeros_like(stat_r)

    @pl.when(is_rim)
    def _():
        for one in edge_copies:
            one.wait_recv()
        sort_edges(edges_r, counts_r, columns, base + rim_row, ROWS)
        fill_bias(columns, bias_r, ROWS)

    for xx in others:
        q_arrival(q, q_recv, xx).wait_recv()

    @pl.when(is_rim)
    def _():
        for xx in others:
            qr_copy(xx).start()

    spread_o.spread()
    rows_to_partner(grid_other).wait_recv()

    def part_copy(xs, d):
        xx = lax.rem(x + d + 1, 4)
        return pltpu.make_async_remote_copy(
            src_ref=part.at[xs, pl.ds(pl.multiple_of(xx * OWN, OWN), OWN), :],
            dst_ref=po.at[x, xs],
            send_sem=po_send.at[d, xs], recv_sem=po_recv.at[x, xs],
            device_id={"mp": 2 * xx + c}, device_id_type=MESH,
        )

    rim_slot = jnp.where(is_top, 4, 5)

    def rim_copy(xs, xx):
        return pltpu.make_async_remote_copy(
            src_ref=part_r.at[xs, pl.ds(xx * OWN, OWN), :],
            dst_ref=po.at[rim_slot, xs],
            send_sem=ro_send.at[xx, xs], recv_sem=po_recv.at[rim_slot, xs],
            device_id={"band": rim_to, "mp": 2 * xx + c}, device_id_type=MESH,
        )

    def stat_copy(d):
        xx = lax.rem(x + d + 1, 4)
        return pltpu.make_async_remote_copy(
            src_ref=stat_t.at[lax.div(xx, 2)], dst_ref=st.at[x],
            send_sem=st_send.at[d], recv_sem=st_recv.at[x],
            device_id={"mp": 2 * xx + c}, device_id_type=MESH,
        )

    def rim_stat_copy(xx):
        return pltpu.make_async_remote_copy(
            src_ref=stat_rt.at[xx // 2], dst_ref=st.at[rim_slot],
            send_sem=rs_send.at[xx], recv_sem=st_recv.at[rim_slot],
            device_id={"band": rim_to, "mp": 2 * xx + c}, device_id_type=MESH,
        )

    chunk = 128

    def attend(xs, q_ref, bias_ref, part_ref, stat_ref, first_row, width):
        def block(i, carry):
            at = pl.ds(pl.multiple_of(i * chunk, chunk), chunk)
            span = pl.ds(pl.multiple_of(first_row, ROWS), width)
            result, sums = two_heads(q_ref[xs, at, :], keys[span, :], vals[span, :], bias_ref[at, :])
            part_ref[xs, at, :] = result
            lane = lax.broadcasted_iota(jnp.int32, (chunk, 128), 1)
            old = stat_ref[at, :]
            old = jnp.where(lane == 2 * xs, sums[0], old)
            stat_ref[at, :] = jnp.where(lane == 2 * xs + 1, sums[1], old)
            return carry

        lax.fori_loop(0, NODES // chunk, block, 0, unroll=True)

    def slice_of(xs):
        def project(i, inner):
            at = pl.ds(pl.multiple_of(i * ROWS, ROWS), ROWS)
            both = jnp.dot(normed[at, :], w[xs], preferred_element_type=F32).astype(BF16)
            keys[at, :] = both[:, :COLS]
            vals[at, 0:COLS] = both[:, COLS:]
            return inner

        lax.fori_loop(0, 2, project, 0)

        @pl.when(is_rim)
        def _():
            q_arrival(qr, qr_recv, xs).wait_recv()
            attend(xs, qr, bias_r, part_r, stat_r, rim_row, ROWS)
            for xx in range(4):
                rim_copy(xs, xx).start()

        attend(xs, q, bias, part, stat, 0, 2 * ROWS)
        for d in range(3):
            part_copy(xs, d).start()

    def head_step(j, carry):
        xs = lax.rem(x + jnp.where(j == 1, 3, jnp.where(j == 2, 1, 2)), 4)
        for k in range(3):

            @pl.when(j == k + 1)
            def _():
                weight_wait(k)

        @pl.when(j == 2)
        def _():
            weight_relay(2, 0)
            weight_relay(2, 1)

        slice_of(xs)
        return carry

    local[0].wait()
    local[1].wait()
    weight_relay(0, 1)
    weight_relay(1, 1)
    slice_of(x)
    lax.fori_loop(1, 4, head_step, 0)

    for half in range(2):
        stat_t[half] = stat[half * 128 : half * 128 + 128, :].T[0:8]
    for d in range(3):
        stat_copy(d).start()

    @pl.when(is_rim)
    def _():
        for half in range(2):
            stat_rt[half] = stat_r[half * 128 : half * 128 + 128, :].T[0:8]
        for xx in range(4):
            rim_stat_copy(xx).start()

    spread_p.spread()
    mine = pl.ds(pl.multiple_of(x * OWN, OWN), OWN)
    st[x] = stat_t[lax.div(x, 2)]
    for xs in range(4):
        po[x, xs] = part[xs, mine, :]

    def arrivals(i):
        for xs in range(4):
            pltpu.make_async_remote_copy(
                src_ref=po.at[i, xs], dst_ref=po.at[i, xs],
                send_sem=po_send.at[0, xs], recv_sem=po_recv.at[i, xs],
                device_id={"mp": m}, device_id_type=MESH,
            ).wait_recv()
        pltpu.make_async_remote_copy(
            src_ref=st.at[i], dst_ref=st.at[i], send_sem=st_send.at[0], recv_sem=st_recv.at[i],
            device_id={"mp": m}, device_id_type=MESH,
        ).wait_recv()

    for d in range(3):
        arrivals(lax.rem(x + d + 1, 4))
    arrivals(4)
    arrivals(5)

    top = st[0]
    for i in range(1, 6):
        top = jnp.maximum(top, st[i])
    shares = [jnp.exp(st[i] - top) for i in range(6)]
    whole = shares[0]
    for i in range(1, 6):
        whole = whole + shares[i]
    shares = [one / whole for one in shares]
    spare[...] = jnp.concatenate(shares + [jnp.zeros((128 - 48, 128), F32)], axis=0).T
    share = spare[pl.ds(pl.multiple_of(lax.rem(x, 2) * OWN, OWN), OWN), :]
    first = lax.broadcasted_iota(jnp.int32, (OWN, COLS), 1) < HALF
    for xs in range(4):
        total = jnp.zeros((OWN, COLS), F32)
        for i in range(6):
            at = i * 8 + 2 * xs
            left = jnp.broadcast_to(share[:, at : at + 1], (OWN, COLS))
            right = jnp.broadcast_to(share[:, at + 1 : at + 2], (OWN, COLS))
            total = total + jnp.where(first, left, right) * po[i, xs].astype(F32)
        heads[mine, at_cols(c * 512 + xs * COLS)] = total.astype(BF16)

    ring_h.start()
    ring_h.relay()
    local[3].wait()
    spread_o.collect()

    def half_product(left, right, cc, at):
        return jnp.dot(
            left[:, pl.ds(pl.multiple_of(cc * 512, 512), 512)],
            right[pl.ds(cc * 4, 4), :, at].reshape(512, 256),
            preferred_element_type=F32,
        )

    def latent_first(n, carry):
        at = pl.ds(pl.multiple_of(n * 256, 256), 256)
        latent[:, at] = hidden[:, at].astype(F32) + half_product(heads, wo_all, c, at)
        return carry

    def latent_second(n, carry):
        at = pl.ds(pl.multiple_of(n * 256, 256), 256)
        latent[:, at] = latent[:, at] + half_product(heads, wo_all, 1 - c, at)
        return carry

    lax.fori_loop(0, 4, latent_first, 0, unroll=True)
    ring_h.from_partner()
    spread_o.from_partner()
    lax.fori_loop(0, 4, latent_second, 0, unroll=True)

    def latent_norm(i, carry):
        at = pl.ds(pl.multiple_of(i * 64, 64), 64)
        node[at, :] = norm_rows(latent[at, :], proc_gain[...]).astype(BF16)
        return carry

    lax.fori_loop(0, NODES // 64, latent_norm, 0)

    local[5].wait()
    local[6].wait()
    kvp[WIN : WIN + NODES, :] = jnp.dot(
        node[...], pw[...], preferred_element_type=F32
    ).astype(BF16)

    def kv_copy(k):
        source, target = ((NODES, 0), (WIN, WIN + NODES))[k]
        return pltpu.make_async_remote_copy(
            src_ref=kvp.at[pl.ds(source, WIN), :], dst_ref=kvp.at[pl.ds(target, WIN), :],
            send_sem=kv_send.at[k], recv_sem=kv_recv.at[k],
            device_id={"band": (up, down)[k], "mp": m}, device_id_type=MESH,
        )

    for k in range(2):
        kv_copy(k).start()
    local[7].wait()
    query = jnp.dot(node[...], pq[...], preferred_element_type=F32).astype(BF16) * BF16(0.125)
    local[4].wait()
    spread_p.collect()
    for k in range(2):
        kv_copy(k).wait_recv()

    span = NODES + 2 * WIN
    vals[0:span, 0:COLS] = kvp[:, COLS:]
    i = lax.broadcasted_iota(jnp.int32, (NODES, span), 0)
    j = lax.broadcasted_iota(jnp.int32, (NODES, span), 1)
    other = b * NODES - WIN + j
    valid = (jnp.abs(i + WIN - j) <= WIN) & (other >= 0) & (other < bands * NODES)
    result, _ = two_heads(query, kvp[:, 0:COLS], vals[0:span, :], jnp.where(valid, 0.0, NEG))
    heads2[:, at_cols(slot * COLS)] = result

    ring_g.start()
    for mat in range(2):
        for k in range(3):
            for s in range(2):
                weight_x(mat, k, s).wait_send()
                for t in range(2):
                    weight_y(mat, k, s, t, parity).wait_send()
    for one in (spread_o, spread_p, ring_h):
        one.drain()
    rows_to_partner(grid_own).wait_send()
    for d in range(3):
        q_copy(d).wait_send()
        stat_copy(d).wait_send()
        for xs in range(4):
            part_copy(xs, d).wait_send()
    for k in range(2):
        kv_copy(k).wait_send()

    @pl.when(is_rim)
    def _():
        for one in edge_copies:
            one.wait_send()
        for xx in range(4):
            qr_copy(xx).wait_send()
            rim_stat_copy(xx).wait_send()
            for xs in range(4):
                rim_copy(xs, xx).wait_send()

    ring_g.relay()

    def mixed_first(n, carry):
        at = pl.ds(pl.multiple_of(n * 256, 256), 256)
        latent[:, at] = latent[:, at] + half_product(heads2, pwo_all, c, at)
        return carry

    def mixed_second(n, carry):
        at = pl.ds(pl.multiple_of(n * 256, 256), 256)
        node[:, at] = (latent[:, at] + half_product(heads2, pwo_all, 1 - c, at)).astype(BF16)
        pltpu.make_async_copy(node.at[:, at], out.at[:, at], out_sem.at[n]).start()
        return carry

    lax.fori_loop(0, 4, mixed_first, 0, unroll=True)
    ring_g.from_partner()
    spread_p.from_partner()
    lax.fori_loop(0, 4, mixed_second, 0, unroll=True)

    ring_g.drain()
    for n in range(4):
        at = pl.ds(n * 256, 256)
        pltpu.make_async_copy(node.at[:, at], out.at[:, at], out_sem.at[n]).wait()


def solution(mesh):
    bands = mesh.shape["band"]
    ring = RING if bands % RING == 0 else 2
    layers = bands // ring

    def step(
        grid_latent, grid_gain, hidden_in, hid_gain, enc_wq, enc_wk, enc_wv, enc_wo,
        enc_edges, enc_counts, proc_gain, proc_wq, proc_wk, proc_wv, proc_wo,
    ):
        counts = enc_counts.reshape(1, NODES)
        edges = enc_edges.T
        hbm = pl.BlockSpec(memory_space=pl.ANY)
        vmem = pl.BlockSpec(memory_space=pltpu.VMEM)
        dma = pltpu.SemaphoreType.DMA
        spread_sems = lambda n: [dma((3,)), dma((4,)), dma((3, n)), dma((4, n)), dma((2,))]
        ring_sems = [dma((7,)), dma((2, 4))]
        return pl.pallas_call(
            functools.partial(kernel, bands, ring),
            out_shape=jax.ShapeDtypeStruct((NODES, D), BF16),
            in_specs=[hbm] * 10 + [vmem] * 7,
            out_specs=hbm,
            scratch_shapes=[
                pltpu.VMEM((ROWS, D), BF16),
                pltpu.VMEM((2 * ROWS, D), BF16),
                pltpu.VMEM((NODES, D), BF16),
                pltpu.VMEM((4, D, 2 * COLS), BF16),
                pltpu.VMEM((4, NODES, COLS), BF16),
                pltpu.VMEM((4, NODES, COLS), BF16),
                pltpu.VMEM((2 * ROWS, COLS), BF16),
                pltpu.VMEM((2 * ROWS, 2 * COLS), BF16),
                pltpu.VMEM((NODES, 2 * ROWS), F32),
                pltpu.VMEM((NODES, ROWS), F32),
                pltpu.VMEM((SLOTS, NODES), jnp.int32),
                pltpu.VMEM((1, NODES), jnp.int32),
                pltpu.VMEM((NODES, COLS), F32),
                pltpu.VMEM((4, NODES, COLS), BF16),
                pltpu.VMEM((NODES, 128), F32),
                pltpu.VMEM((2, 8, 128), F32),
                pltpu.VMEM((4, NODES, COLS), BF16),
                pltpu.VMEM((NODES, 128), F32),
                pltpu.VMEM((2, 8, 128), F32),
                pltpu.VMEM((128, 128), F32),
                pltpu.VMEM((6, 4, OWN, COLS), BF16),
                pltpu.VMEM((6, 8, 128), F32),
                pltpu.VMEM((NODES, D), BF16),
                pltpu.VMEM((8, COLS, D), BF16),
                pltpu.VMEM((8, COLS, D), BF16),
                pltpu.VMEM((NODES, D), F32),
                pltpu.VMEM((D, 2 * COLS), BF16),
                pltpu.VMEM((D, COLS), BF16),
                pltpu.VMEM((NODES + 2 * WIN, 2 * COLS), BF16),
                pltpu.VMEM((NODES, D), BF16),
            ]
            + [dma((2, 3, 2)), dma((2, 4, 2)), dma((2, 3, 2, 2)), dma((2, 4, 2, 2))]
            + spread_sems(layers) * 2
            + ring_sems * 2
            + [
                dma((8,)),
                dma((2,)),
                dma((2, 2)),
                dma((3,)), dma((4,)),
                dma((4,)), dma((4,)),
                dma((4,)),
                dma((3, 4)), dma((6, 4)),
                dma((3,)), dma((6,)),
                dma((4, 4)), dma((4,)),
                dma((2,)), dma((2,)),
            ],
            compiler_params=pltpu.CompilerParams(
                collective_id=0, has_side_effects=True, vmem_limit_bytes=60 * 1024 * 1024
            ),
        )(
            grid_latent, enc_wk, enc_wv, enc_wo, proc_wk, proc_wv, proc_wq, proc_wo, edges, counts,
            grid_gain.reshape(1, D), hidden_in, hid_gain.reshape(1, D), enc_wq, edges, counts,
            proc_gain.reshape(1, D),
        )

    return jax.shard_map(
        step,
        mesh=mesh,
        in_specs=(
            P(("band", "mp"), None), P(), P("band", None), P(),
            P(None, "mp"), P(None, "mp"), P(None, "mp"), P("mp", None),
            P("band", None), P("band"), P(),
            P(None, "mp"), P(None, "mp"), P(None, "mp"), P("mp", None),
        ),
        out_specs=P("band", None),
        check_vma=False,
    )
```

```python
import functools

import jax
import jax.numpy as jnp
from jax import lax
from jax.experimental import pallas as pl
from jax.experimental.pallas import tpu as pltpu
from jax.sharding import PartitionSpec as P

MESH = pl.DeviceIdType.MESH
EPSILON = 1e-05
NEG = -1e30
F32 = jnp.float32
BF16 = jnp.bfloat16

D = 1024
CHIPS = 4
ROWS = 512
NODES = 256
SLOTS = 32
WIN = 128
COLS = 128
HALF = 64
OWN = NODES // CHIPS
RING = 8


def norm_rows(values, gain):
    values = values.astype(F32)
    center = values - jnp.mean(values, axis=-1, keepdims=True)
    spread = jnp.mean(center * center, axis=-1, keepdims=True)
    return center * lax.rsqrt(spread + EPSILON) * gain


def at_cols(start):
    return pl.ds(pl.multiple_of(start, COLS), COLS)


class Ring:
    def __init__(self, place, send, recv, x, c):
        self.place, self.send, self.recv, self.x, self.c = place, send, recv, x, c
        self.others = [lax.rem(x + d, 4) for d in (3, 1, 2)]

    def copy(self, c, x, kind, device):
        ref = self.place(c, x)
        return pltpu.make_async_remote_copy(
            src_ref=ref, dst_ref=ref, send_sem=self.send.at[kind], recv_sem=self.recv.at[c, x],
            device_id={"mp": device}, device_id_type=MESH,
        )

    def sends(self):
        return [self.copy(self.c, self.x, k, 2 * xx + self.c) for k, xx in enumerate(self.others)]

    def to_partner(self, k):
        xx = self.x if k == 3 else self.others[k]
        return self.copy(self.c, xx, 3 + k, 2 * self.x + 1 - self.c)

    def start(self):
        for one in self.sends():
            one.start()
        self.to_partner(3).start()

    def relay(self):
        for k, xx in enumerate(self.others):
            self.copy(self.c, xx, k, 2 * xx + self.c).wait_recv()
            self.to_partner(k).start()

    def from_partner(self):
        for xx in range(4):
            self.copy(1 - self.c, xx, 0, 2 * self.x + 1 - self.c).wait_recv()

    def drain(self):
        for one in self.sends():
            one.wait_send()
        for k in range(4):
            self.to_partner(k).wait_send()


class Spread:
    def __init__(self, source, held, n, index, band_of, x, c, m, sems):
        self.source, self.held, self.n, self.index, self.band_of = source, held, n, index, band_of
        self.x, self.c, self.m = x, c, m
        self.x_send, self.x_recv, self.r_send, self.r_recv, self.p_sem = sems
        self.others = [lax.rem(x + d, 4) for d in (3, 1, 2)]
        self.rows = COLS // n

    def at(self, i):
        return pl.ds(pl.multiple_of(i * self.rows, self.rows), self.rows)

    def over_x(self, k):
        return pltpu.make_async_remote_copy(
            src_ref=self.source.at[self.at(self.index), :],
            dst_ref=self.held.at[self.c * 4 + self.x, self.at(self.index), :],
            send_sem=self.x_send.at[k], recv_sem=self.x_recv.at[self.x],
            device_id={"mp": 2 * self.others[k] + self.c}, device_id_type=MESH,
        )

    def piece(self, k, i, sem, recv, band):
        ref = self.held.at[self.c * 4 + self.others[k], self.at(i), :]
        return pltpu.make_async_remote_copy(
            src_ref=ref, dst_ref=ref, send_sem=sem, recv_sem=recv,
            device_id={"band": band, "mp": self.m}, device_id_type=MESH,
        )

    def along(self, k, d):
        i = lax.rem(self.index + d, self.n)
        return self.piece(
            k, self.index, self.r_send.at[k, d], self.r_recv.at[self.others[k], self.index], self.band_of(i)
        )

    def start(self):
        for k in range(3):
            self.over_x(k).start()

    def spread(self):
        for k in range(3):
            self.piece(
                k, self.index, self.r_send.at[k, 0], self.x_recv.at[self.others[k]], self.band_of(self.index)
            ).wait_recv()
        for d in range(1, self.n):
            for k in range(3):
                self.along(k, d).start()

    def to_partner(self, c):
        ref = self.held.at[pl.ds(c * 4, 4)]
        return pltpu.make_async_remote_copy(
            src_ref=ref, dst_ref=ref, send_sem=self.p_sem.at[0], recv_sem=self.p_sem.at[1],
            device_id={"mp": 2 * self.x + 1 - self.c}, device_id_type=MESH,
        )

    def collect(self):
        for k in range(3):
            for d in range(1, self.n):
                i = lax.rem(self.index + d, self.n)
                self.piece(
                    k, i, self.r_send.at[k, 0], self.r_recv.at[self.others[k], i], self.band_of(i)
                ).wait_recv()
        self.to_partner(self.c).start()

    def from_partner(self):
        self.to_partner(1 - self.c).wait_recv()

    def drain(self):
        for k in range(3):
            self.over_x(k).wait_send()
            for d in range(1, self.n):
                self.along(k, d).wait_send()
        self.to_partner(self.c).wait_send()


def code_of(index):
    high = jnp.clip(index >> 7, 0, 7)
    return ((COLS + (index & 127)) << high).astype(F32)


def sort_edges(edges_ref, counts_ref, columns_ref, base, width):
    slot = lax.broadcasted_iota(jnp.int32, (SLOTS, NODES), 0)
    index = edges_ref[...] - base
    live = (slot < counts_ref[...]) & (index >= 0) & (index < width)
    codes = jnp.where(live, code_of(index), -1.0)
    columns_ref[...] = jnp.concatenate([codes, jnp.full((COLS - SLOTS, NODES), -1.0, F32)], axis=0).T


def fill_bias(columns_ref, bias_ref, width):
    step = 16
    lane = lax.broadcasted_iota(jnp.int32, (step, COLS), 1)
    columns = [code_of(lane + k * COLS).astype(BF16) for k in range(width // COLS)]

    def block(i, carry):
        at = pl.ds(pl.multiple_of(i * step, step), step)
        edges = columns_ref[at, :]
        totals = [jnp.zeros((step, COLS), BF16) for _ in columns]
        for s in range(SLOTS):
            edge = jnp.broadcast_to(edges[:, s : s + 1], (step, COLS)).astype(BF16)
            totals = [
                total + jnp.where(edge == column, BF16(1), BF16(0)) for total, column in zip(totals, columns)
            ]
        for k, total in enumerate(totals):
            total = total.astype(F32)
            bias_ref[at, k * COLS : (k + 1) * COLS] = jnp.where(
                total > 0.0, jnp.log(jnp.maximum(total, 1.0)), NEG
            )
        return carry

    lax.fori_loop(0, NODES // step, block, 0)


def two_heads(query, keys, values, bias):
    first = lax.broadcasted_iota(jnp.int32, query.shape, 1) < HALF
    outs, sums = [], []
    for h in range(2):
        q = jnp.where(first if h == 0 else jnp.logical_not(first), query, jnp.zeros_like(query))
        scores = lax.dot_general(q, keys, (((1,), (1,)), ((), ())), preferred_element_type=F32) + bias
        top = jnp.max(scores, axis=1, keepdims=True)
        weights = jnp.exp(scores - top).astype(BF16)
        both = jnp.dot(weights, values, preferred_element_type=F32)
        total = both[:, COLS:]
        outs.append(both[:, :COLS] / total)
        sums.append(top + jnp.log(total))
    return jnp.where(first, outs[0], outs[1]).astype(BF16), sums


def kernel(
    bands, ring,
    grid, wk, wv, wo, pwk, pwv, pwq, pwo, edges_hbm, counts_hbm,
    grid_gain, hidden, hid_gain, wq, edges, counts, proc_gain,
    out,
    raw, normed, node, w, q, qr, keys, vals, bias, bias_r, edges_r, counts_r, columns,
    part, stat, stat_t, part_r, stat_r, stat_rt, spare, po, st, heads, wo_all, pwo_all, latent, pw, pq, kvp, heads2,
    wx_send, wx_recv, wy_send, wy_recv,
    o0, o1, o2, o3, o4, p0, p1, p2, p3, p4, hs, hr, gs, gr,
    loc, grid_sem, edge_sem, q_send, q_recv, qr_send, qr_recv, out_sem,
    po_send, po_recv, st_send, st_recv, ro_send, rs_send, kv_send, kv_recv,
):
    b, m = lax.axis_index("band"), lax.axis_index("mp")
    x, c = lax.div(m, 2), lax.rem(m, 2)
    up, down = lax.rem(b + 1, bands), lax.rem(b + bands - 1, bands)
    is_top, is_low = x == 3, x == 0
    is_rim = jnp.logical_or(is_top, is_low)

    layers = bands // ring
    y, z = lax.rem(b, ring), lax.div(b, ring)
    parity = lax.rem(y, 2)

    def band_in_y(i):
        return z * ring + i

    def band_in_z(i):
        return i * ring + y

    ahead, behind = band_in_y(lax.rem(y + 1, ring)), band_in_y(lax.rem(y + ring - 1, ring))

    barrier = pltpu.get_barrier_semaphore()

    def greet(device):
        pl.semaphore_signal(barrier, inc=1, device_id=device, device_id_type=MESH)

    for d in range(1, 8):
        greet({"mp": lax.rem(m + d, 8)})
    for band in (up, down):
        for d in range(4):
            greet({"band": band, "mp": 2 * d + c})
    for d in range(1, ring):
        greet({"band": band_in_y(lax.rem(y + d, ring)), "mp": m})
    for d in range(1, layers):
        greet({"band": band_in_z(lax.rem(z + d, layers)), "mp": m})

    slot = c * 4 + x
    local = [
        pltpu.make_async_copy(wk, w.at[x, :, 0:COLS], loc.at[0]),
        pltpu.make_async_copy(wv, w.at[x, :, COLS:], loc.at[1]),
        pltpu.make_async_copy(grid, raw, loc.at[2]),
        pltpu.make_async_copy(wo, wo_all.at[slot], loc.at[3]),
        pltpu.make_async_copy(pwo, pwo_all.at[slot], loc.at[4]),
        pltpu.make_async_copy(pwk, pw.at[:, 0:COLS], loc.at[5]),
        pltpu.make_async_copy(pwv, pw.at[:, COLS:], loc.at[6]),
        pltpu.make_async_copy(pwq, pq, loc.at[7]),
    ]
    for one in local:
        one.start()
    def node_block(i, carry):
        at = pl.ds(pl.multiple_of(i * 64, 64), 64)
        node[at, :] = norm_rows(hidden[at, :], hid_gain[...]).astype(BF16)
        return carry

    lax.fori_loop(0, NODES // 64, node_block, 0)
    q[x] = jnp.dot(node[...], wq[...], preferred_element_type=F32).astype(BF16) * BF16(0.125)

    def grid_block(i, carry):
        at = pl.ds(pl.multiple_of(i * 64, 64), 64)
        normed[pl.ds(pl.multiple_of(c * ROWS + i * 64, 64), 64), :] = norm_rows(raw[at, :], grid_gain[...]).astype(BF16)
        return carry

    local[2].wait()
    lax.fori_loop(0, ROWS // 64, grid_block, 0)
    pl.semaphore_wait(barrier, 13 + ring + layers)


    others = [lax.rem(x + d, 4) for d in (3, 1, 2)]

    def weight_part(xx, mat, row, count):
        return w.at[xx, pl.ds(pl.multiple_of(row, 128), count), pl.ds(mat * COLS, COLS)]

    def weight_x(mat, k, s):
        row = parity * 512 + s * 256
        return pltpu.make_async_remote_copy(
            src_ref=(wk, wv)[mat].at[pl.ds(pl.multiple_of(row, 256), 256), :],
            dst_ref=weight_part(x, mat, row, 256),
            send_sem=wx_send.at[mat, k, s], recv_sem=wx_recv.at[mat, x, s],
            device_id={"mp": 2 * others[k] + c}, device_id_type=MESH,
        )

    def weight_y(mat, k, s, t, half):
        ref = weight_part(others[k], mat, half * 512 + s * 256 + t * 128, 128)
        return pltpu.make_async_remote_copy(
            src_ref=ref, dst_ref=ref,
            send_sem=wy_send.at[mat, k, s, t], recv_sem=wy_recv.at[mat, others[k], s, t],
            device_id={"band": (ahead, behind)[t], "mp": m}, device_id_type=MESH,
        )

    def weight_relay(k, s):
        for mat in range(2):
            ref = weight_part(others[k], mat, parity * 512 + s * 256, 256)
            pltpu.make_async_remote_copy(
                src_ref=ref, dst_ref=ref,
                send_sem=wx_send.at[mat, k, s], recv_sem=wx_recv.at[mat, others[k], s],
                device_id={"mp": 2 * others[k] + c}, device_id_type=MESH,
            ).wait_recv()
            for t in range(2):
                weight_y(mat, k, s, t, parity).start()

    def weight_wait(k):
        for mat in range(2):
            for s in range(2):
                for t in range(2):
                    weight_y(mat, k, s, t, 1 - parity).wait_recv()

    spread_o = Spread(wo, wo_all, layers, z, band_in_z, x, c, m, (o0, o1, o2, o3, o4))
    spread_p = Spread(pwo, pwo_all, layers, z, band_in_z, x, c, m, (p0, p1, p2, p3, p4))

    def head_piece(cc, xx):
        return heads.at[
            pl.ds(pl.multiple_of(xx * OWN, OWN), OWN), pl.ds(pl.multiple_of(cc * 512, 512), 512)
        ]

    def out_piece(cc, xx):
        return heads2.at[:, at_cols((cc * 4 + xx) * COLS)]

    ring_h = Ring(head_piece, hs, hr, x, c)
    ring_g = Ring(out_piece, gs, gr, x, c)

    grid_own = pl.ds(pl.multiple_of(c * ROWS, ROWS), ROWS)
    grid_other = pl.ds(pl.multiple_of((1 - c) * ROWS, ROWS), ROWS)

    def rows_to_partner(at):
        return pltpu.make_async_remote_copy(
            src_ref=normed.at[at, :], dst_ref=normed.at[at, :], send_sem=grid_sem.at[0], recv_sem=grid_sem.at[1],
            device_id={"mp": 2 * x + 1 - c}, device_id_type=MESH,
        )

    def rim_input(source, target, k, band):
        return pltpu.make_async_remote_copy(
            src_ref=source, dst_ref=target, send_sem=edge_sem.at[0, k], recv_sem=edge_sem.at[1, k],
            device_id={"band": band, "mp": m}, device_id_type=MESH,
        )

    rim_from = jnp.where(is_top, down, up)
    rim_to = jnp.where(is_top, up, down)
    edge_copies = [
        rim_input(edges_hbm, edges_r, 0, rim_from),
        rim_input(counts_hbm, counts_r, 1, rim_from),
    ]

    @pl.when(is_rim)
    def _():
        for one in edge_copies:
            one.start()

    def q_copy(d):
        return pltpu.make_async_remote_copy(
            src_ref=q.at[x], dst_ref=q.at[x], send_sem=q_send.at[d], recv_sem=q_recv.at[x],
            device_id={"mp": 2 * lax.rem(x + d + 1, 4) + c}, device_id_type=MESH,
        )

    outer = jnp.where(is_top, down, up)

    def qr_copy(xx):
        return pltpu.make_async_remote_copy(
            src_ref=q.at[xx], dst_ref=qr.at[xx], send_sem=qr_send.at[xx], recv_sem=qr_recv.at[xx],
            device_id={"band": outer, "mp": m}, device_id_type=MESH,
        )

    def q_arrival(ref, sems, xx):
        return pltpu.make_async_remote_copy(
            src_ref=ref.at[xx], dst_ref=ref.at[xx], send_sem=q_send.at[0], recv_sem=sems.at[xx],
            device_id={"mp": 2 * xx + c}, device_id_type=MESH,
        )

    for mat in range(2):
        for k in range(2):
            weight_x(mat, k, 0).start()
    rows_to_partner(grid_own).start()
    for d in range(3):
        q_copy(d).start()

    @pl.when(is_rim)
    def _():
        qr_copy(x).start()

    spread_o.start()
    for mat in range(2):
        for k in range(2):
            weight_x(mat, k, 1).start()
    for mat in range(2):
        for s in range(2):
            weight_x(mat, 2, s).start()
    spread_p.start()

    base = b * (8 * ROWS) + x * (2 * ROWS)
    rim_row = jnp.where(is_top, ROWS, 0)
    sort_edges(edges, counts, columns, base, 2 * ROWS)
    fill_bias(columns, bias, 2 * ROWS)
    weight_relay(0, 0)
    weight_relay(1, 0)
    vals[:, COLS:] = jnp.ones((2 * ROWS, COLS), BF16)
    stat[...] = jnp.zeros_like(stat)
    stat_r[...] = jnp.zeros_like(stat_r)

    @pl.when(is_rim)
    def _():
        for one in edge_copies:
            one.wait_recv()
        sort_edges(edges_r, counts_r, columns, base + rim_row, ROWS)
        fill_bias(columns, bias_r, ROWS)

    for xx in others:
        q_arrival(q, q_recv, xx).wait_recv()

    @pl.when(is_rim)
    def _():
        for xx in others:
            qr_copy(xx).start()

    spread_o.spread()
    rows_to_partner(grid_other).wait_recv()

    def part_copy(xs, d):
        xx = lax.rem(x + d + 1, 4)
        return pltpu.make_async_remote_copy(
            src_ref=part.at[xs, pl.ds(pl.multiple_of(xx * OWN, OWN), OWN), :],
            dst_ref=po.at[x, xs],
            send_sem=po_send.at[d, xs], recv_sem=po_recv.at[x, xs],
            device_id={"mp": 2 * xx + c}, device_id_type=MESH,
        )

    rim_slot = jnp.where(is_top, 4, 5)

    def rim_copy(xs, xx):
        return pltpu.make_async_remote_copy(
            src_ref=part_r.at[xs, pl.ds(xx * OWN, OWN), :],
            dst_ref=po.at[rim_slot, xs],
            send_sem=ro_send.at[xx, xs], recv_sem=po_recv.at[rim_slot, xs],
            device_id={"band": rim_to, "mp": 2 * xx + c}, device_id_type=MESH,
        )

    def stat_copy(d):
        xx = lax.rem(x + d + 1, 4)
        return pltpu.make_async_remote_copy(
            src_ref=stat_t.at[lax.div(xx, 2)], dst_ref=st.at[x],
            send_sem=st_send.at[d], recv_sem=st_recv.at[x],
            device_id={"mp": 2 * xx + c}, device_id_type=MESH,
        )

    def rim_stat_copy(xx):
        return pltpu.make_async_remote_copy(
            src_ref=stat_rt.at[xx // 2], dst_ref=st.at[rim_slot],
            send_sem=rs_send.at[xx], recv_sem=st_recv.at[rim_slot],
            device_id={"band": rim_to, "mp": 2 * xx + c}, device_id_type=MESH,
        )

    chunk = 128

    def attend(xs, q_ref, bias_ref, part_ref, stat_ref, first_row, width):
        def block(i, carry):
            at = pl.ds(pl.multiple_of(i * chunk, chunk), chunk)
            span = pl.ds(pl.multiple_of(first_row, ROWS), width)
            result, sums = two_heads(q_ref[xs, at, :], keys[span, :], vals[span, :], bias_ref[at, :])
            part_ref[xs, at, :] = result
            lane = lax.broadcasted_iota(jnp.int32, (chunk, 128), 1)
            old = stat_ref[at, :]
            old = jnp.where(lane == 2 * xs, sums[0], old)
            stat_ref[at, :] = jnp.where(lane == 2 * xs + 1, sums[1], old)
            return carry

        lax.fori_loop(0, NODES // chunk, block, 0, unroll=True)

    def slice_of(xs):
        def project(i, inner):
            at = pl.ds(pl.multiple_of(i * ROWS, ROWS), ROWS)
            both = jnp.dot(normed[at, :], w[xs], preferred_element_type=F32).astype(BF16)
            keys[at, :] = both[:, :COLS]
            vals[at, 0:COLS] = both[:, COLS:]
            return inner

        lax.fori_loop(0, 2, project, 0)

        @pl.when(is_rim)
        def _():
            q_arrival(qr, qr_recv, xs).wait_recv()
            attend(xs, qr, bias_r, part_r, stat_r, rim_row, ROWS)
            for xx in range(4):
                rim_copy(xs, xx).start()

        attend(xs, q, bias, part, stat, 0, 2 * ROWS)
        for d in range(3):
            part_copy(xs, d).start()

    def head_step(j, carry):
        xs = lax.rem(x + jnp.where(j == 1, 3, jnp.where(j == 2, 1, 2)), 4)
        for k in range(3):

            @pl.when(j == k + 1)
            def _():
                weight_wait(k)

        @pl.when(j == 2)
        def _():
            weight_relay(2, 0)
            weight_relay(2, 1)

        slice_of(xs)
        return carry

    local[0].wait()
    local[1].wait()
    weight_relay(0, 1)
    slice_of(x)
    weight_relay(1, 1)
    lax.fori_loop(1, 4, head_step, 0)

    for half in range(2):
        stat_t[half] = stat[half * 128 : half * 128 + 128, :].T[0:8]
    for d in range(3):
        stat_copy(d).start()

    @pl.when(is_rim)
    def _():
        for half in range(2):
            stat_rt[half] = stat_r[half * 128 : half * 128 + 128, :].T[0:8]
        for xx in range(4):
            rim_stat_copy(xx).start()

    spread_p.spread()
    mine = pl.ds(pl.multiple_of(x * OWN, OWN), OWN)
    st[x] = stat_t[lax.div(x, 2)]
    for xs in range(4):
        po[x, xs] = part[xs, mine, :]

    def arrivals(i):
        for xs in range(4):
            pltpu.make_async_remote_copy(
                src_ref=po.at[i, xs], dst_ref=po.at[i, xs],
                send_sem=po_send.at[0, xs], recv_sem=po_recv.at[i, xs],
                device_id={"mp": m}, device_id_type=MESH,
            ).wait_recv()
        pltpu.make_async_remote_copy(
            src_ref=st.at[i], dst_ref=st.at[i], send_sem=st_send.at[0], recv_sem=st_recv.at[i],
            device_id={"mp": m}, device_id_type=MESH,
        ).wait_recv()

    for d in range(3):
        arrivals(lax.rem(x + d + 1, 4))
    arrivals(4)
    arrivals(5)

    top = st[0]
    for i in range(1, 6):
        top = jnp.maximum(top, st[i])
    shares = [jnp.exp(st[i] - top) for i in range(6)]
    whole = shares[0]
    for i in range(1, 6):
        whole = whole + shares[i]
    shares = [one / whole for one in shares]
    spare[...] = jnp.concatenate(shares + [jnp.zeros((128 - 48, 128), F32)], axis=0).T
    share = spare[pl.ds(pl.multiple_of(lax.rem(x, 2) * OWN, OWN), OWN), :]
    first = lax.broadcasted_iota(jnp.int32, (OWN, COLS), 1) < HALF
    for xs in range(4):
        total = jnp.zeros((OWN, COLS), F32)
        for i in range(6):
            at = i * 8 + 2 * xs
            left = jnp.broadcast_to(share[:, at : at + 1], (OWN, COLS))
            right = jnp.broadcast_to(share[:, at + 1 : at + 2], (OWN, COLS))
            total = total + jnp.where(first, left, right) * po[i, xs].astype(F32)
        heads[mine, at_cols(c * 512 + xs * COLS)] = total.astype(BF16)

    ring_h.start()
    ring_h.relay()
    local[3].wait()
    spread_o.collect()

    def half_product(left, right, cc, at):
        return jnp.dot(
            left[:, pl.ds(pl.multiple_of(cc * 512, 512), 512)],
            right[pl.ds(cc * 4, 4), :, at].reshape(512, 256),
            preferred_element_type=F32,
        )

    def latent_first(n, carry):
        at = pl.ds(pl.multiple_of(n * 256, 256), 256)
        latent[:, at] = hidden[:, at].astype(F32) + half_product(heads, wo_all, c, at)
        return carry

    def latent_second(n, carry):
        at = pl.ds(pl.multiple_of(n * 256, 256), 256)
        latent[:, at] = latent[:, at] + half_product(heads, wo_all, 1 - c, at)
        return carry

    lax.fori_loop(0, 4, latent_first, 0, unroll=True)
    ring_h.from_partner()
    spread_o.from_partner()
    lax.fori_loop(0, 4, latent_second, 0, unroll=True)

    def latent_norm(i, carry):
        at = pl.ds(pl.multiple_of(i * 64, 64), 64)
        node[at, :] = norm_rows(latent[at, :], proc_gain[...]).astype(BF16)
        return carry

    lax.fori_loop(0, NODES // 64, latent_norm, 0)

    local[5].wait()
    local[6].wait()
    kvp[WIN : WIN + NODES, :] = jnp.dot(
        node[...], pw[...], preferred_element_type=F32
    ).astype(BF16)

    def kv_copy(k):
        source, target = ((NODES, 0), (WIN, WIN + NODES))[k]
        return pltpu.make_async_remote_copy(
            src_ref=kvp.at[pl.ds(source, WIN), :], dst_ref=kvp.at[pl.ds(target, WIN), :],
            send_sem=kv_send.at[k], recv_sem=kv_recv.at[k],
            device_id={"band": (up, down)[k], "mp": m}, device_id_type=MESH,
        )

    for k in range(2):
        kv_copy(k).start()
    local[7].wait()
    query = jnp.dot(node[...], pq[...], preferred_element_type=F32).astype(BF16) * BF16(0.125)
    local[4].wait()
    spread_p.collect()
    for k in range(2):
        kv_copy(k).wait_recv()

    span = NODES + 2 * WIN
    vals[0:span, 0:COLS] = kvp[:, COLS:]
    i = lax.broadcasted_iota(jnp.int32, (NODES, span), 0)
    j = lax.broadcasted_iota(jnp.int32, (NODES, span), 1)
    other = b * NODES - WIN + j
    valid = (jnp.abs(i + WIN - j) <= WIN) & (other >= 0) & (other < bands * NODES)
    result, _ = two_heads(query, kvp[:, 0:COLS], vals[0:span, :], jnp.where(valid, 0.0, NEG))
    heads2[:, at_cols(slot * COLS)] = result

    ring_g.start()
    for mat in range(2):
        for k in range(3):
            for s in range(2):
                weight_x(mat, k, s).wait_send()
                for t in range(2):
                    weight_y(mat, k, s, t, parity).wait_send()
    for one in (spread_o, spread_p, ring_h):
        one.drain()
    rows_to_partner(grid_own).wait_send()
    for d in range(3):
        q_copy(d).wait_send()
        stat_copy(d).wait_send()
        for xs in range(4):
            part_copy(xs, d).wait_send()
    for k in range(2):
        kv_copy(k).wait_send()

    @pl.when(is_rim)
    def _():
        for one in edge_copies:
            one.wait_send()
        for xx in range(4):
            qr_copy(xx).wait_send()
            rim_stat_copy(xx).wait_send()
            for xs in range(4):
                rim_copy(xs, xx).wait_send()

    ring_g.relay()

    def mixed_first(n, carry):
        at = pl.ds(pl.multiple_of(n * 256, 256), 256)
        latent[:, at] = latent[:, at] + half_product(heads2, pwo_all, c, at)
        return carry

    def mixed_second(n, carry):
        at = pl.ds(pl.multiple_of(n * 256, 256), 256)
        node[:, at] = (latent[:, at] + half_product(heads2, pwo_all, 1 - c, at)).astype(BF16)
        pltpu.make_async_copy(node.at[:, at], out.at[:, at], out_sem.at[n]).start()
        return carry

    lax.fori_loop(0, 4, mixed_first, 0, unroll=True)
    ring_g.from_partner()
    spread_p.from_partner()
    lax.fori_loop(0, 4, mixed_second, 0, unroll=True)

    ring_g.drain()
    for n in range(4):
        at = pl.ds(n * 256, 256)
        pltpu.make_async_copy(node.at[:, at], out.at[:, at], out_sem.at[n]).wait()


def solution(mesh):
    bands = mesh.shape["band"]
    ring = RING if bands % RING == 0 else 2
    layers = bands // ring

    def step(
        grid_latent, grid_gain, hidden_in, hid_gain, enc_wq, enc_wk, enc_wv, enc_wo,
        enc_edges, enc_counts, proc_gain, proc_wq, proc_wk, proc_wv, proc_wo,
    ):
        counts = enc_counts.reshape(1, NODES)
        edges = enc_edges.T
        hbm = pl.BlockSpec(memory_space=pl.ANY)
        vmem = pl.BlockSpec(memory_space=pltpu.VMEM)
        dma = pltpu.SemaphoreType.DMA
        spread_sems = lambda n: [dma((3,)), dma((4,)), dma((3, n)), dma((4, n)), dma((2,))]
        ring_sems = [dma((7,)), dma((2, 4))]
        return pl.pallas_call(
            functools.partial(kernel, bands, ring),
            out_shape=jax.ShapeDtypeStruct((NODES, D), BF16),
            in_specs=[hbm] * 10 + [vmem] * 7,
            out_specs=hbm,
            scratch_shapes=[
                pltpu.VMEM((ROWS, D), BF16),
                pltpu.VMEM((2 * ROWS, D), BF16),
                pltpu.VMEM((NODES, D), BF16),
                pltpu.VMEM((4, D, 2 * COLS), BF16),
                pltpu.VMEM((4, NODES, COLS), BF16),
                pltpu.VMEM((4, NODES, COLS), BF16),
                pltpu.VMEM((2 * ROWS, COLS), BF16),
                pltpu.VMEM((2 * ROWS, 2 * COLS), BF16),
                pltpu.VMEM((NODES, 2 * ROWS), F32),
                pltpu.VMEM((NODES, ROWS), F32),
                pltpu.VMEM((SLOTS, NODES), jnp.int32),
                pltpu.VMEM((1, NODES), jnp.int32),
                pltpu.VMEM((NODES, COLS), F32),
                pltpu.VMEM((4, NODES, COLS), BF16),
                pltpu.VMEM((NODES, 128), F32),
                pltpu.VMEM((2, 8, 128), F32),
                pltpu.VMEM((4, NODES, COLS), BF16),
                pltpu.VMEM((NODES, 128), F32),
                pltpu.VMEM((2, 8, 128), F32),
                pltpu.VMEM((128, 128), F32),
                pltpu.VMEM((6, 4, OWN, COLS), BF16),
                pltpu.VMEM((6, 8, 128), F32),
                pltpu.VMEM((NODES, D), BF16),
                pltpu.VMEM((8, COLS, D), BF16),
                pltpu.VMEM((8, COLS, D), BF16),
                pltpu.VMEM((NODES, D), F32),
                pltpu.VMEM((D, 2 * COLS), BF16),
                pltpu.VMEM((D, COLS), BF16),
                pltpu.VMEM((NODES + 2 * WIN, 2 * COLS), BF16),
                pltpu.VMEM((NODES, D), BF16),
            ]
            + [dma((2, 3, 2)), dma((2, 4, 2)), dma((2, 3, 2, 2)), dma((2, 4, 2, 2))]
            + spread_sems(layers) * 2
            + ring_sems * 2
            + [
                dma((8,)),
                dma((2,)),
                dma((2, 2)),
                dma((3,)), dma((4,)),
                dma((4,)), dma((4,)),
                dma((4,)),
                dma((3, 4)), dma((6, 4)),
                dma((3,)), dma((6,)),
                dma((4, 4)), dma((4,)),
                dma((2,)), dma((2,)),
            ],
            compiler_params=pltpu.CompilerParams(
                collective_id=0, has_side_effects=True, vmem_limit_bytes=60 * 1024 * 1024
            ),
        )(
            grid_latent, enc_wk, enc_wv, enc_wo, proc_wk, proc_wv, proc_wq, proc_wo, edges, counts,
            grid_gain.reshape(1, D), hidden_in, hid_gain.reshape(1, D), enc_wq, edges, counts,
            proc_gain.reshape(1, D),
        )

    return jax.shard_map(
        step,
        mesh=mesh,
        in_specs=(
            P(("band", "mp"), None), P(), P("band", None), P(),
            P(None, "mp"), P(None, "mp"), P(None, "mp"), P("mp", None),
            P("band", None), P("band"), P(),
            P(None, "mp"), P(None, "mp"), P(None, "mp"), P("mp", None),
        ),
        out_specs=P("band", None),
        check_vma=False,
    )
```
